32 devices in a mesh: dp: 4 (over y, x), ctx: 8 (over z, core).
Axes of the slice: x: 2, y: 2, z: 4, core: 2. Of those that a mesh axis runs over, the one named last changes fastest.
Arguments:
- tokens: bfloat16 [4, 2048, 1536], P('dp', 'ctx'), may hold values from -40 to 40, as said below
- segments: int32 [4, 2048], P('dp'), may hold values from 0 to 1, never falling along the last dimension, each value on 1 to 1536 neighbouring positions
- w_query: bfloat16 [1536, 1536], replicated, as said below
- w_keyval: bfloat16 [1536, 512], replicated, as said below
- grad_context: bfloat16 [4, 2048, 1536], P('dp', 'ctx'), may hold values from -6 to 6
Outputs:
- context: bfloat16 [4, 2048, 1536], P('dp', 'ctx')
- grad_tokens: bfloat16 [4, 2048, 1536], P('dp', 'ctx')
- grad_query_w: bfloat16 [1536, 1536], P('ctx')
- grad_keyval_w: bfloat16 [1536, 512], P('ctx')
The draws below stay inside these ranges and needn't reach their ends.
Inputs may be any that keep to these rules, and one draw needn't show every extreme that they name: `segments`: document numbers never fall along a sequence; a document covers at most 1536 positions. `tokens`: activations of order one. `w_query`: a weight matrix of fan-in 1536. `w_keyval`: a weight matrix of fan-in 1536.
All inputs are finite; a program needn't handle non-finite values.
Results may differ from the reference program's by a relative error of at most 0.03.
The reference program's roundings to bfloat16 on the way (of `queries`, `keyval`, `probs_low`, `grad_scores`, `grad_queries` and `grad_keyval`) count: a program that leaves them out, or rounds other values in their place, can miss the bound.
Values may be sent and summed in bfloat16 or wider, within the bound.
A program may use at most 128 MiB of HBM per device.

```python
import math
import jax
import jax.numpy as jnp
import numpy as np
from jax import lax

D = 1536
HEADS = 12
KV_HEADS = 2
HEAD_DIM = 128
WINDOW = 512
BLOCK = 128
TOK_DEV = 256
GROUPS = 4
SEQ = 2048
KV_COLS = 512
DOCS = 2
MOST = 1536


def draw_tokens(key, part):
    base = jax.random.fold_in(key, 11)
    first = jax.random.fold_in(base, 0)
    fifth = jax.random.fold_in(base, 4)
    values = jnp.clip(jax.random.normal(first, (GROUPS, SEQ, D), jnp.float32), -6.0, 6.0)
    block_count = SEQ // TOK_DEV
    pairing = jax.random.permutation(fifth, block_count)
    row_block = jnp.arange(SEQ, dtype=jnp.int32) // TOK_DEV
    col_block = jnp.arange(D, dtype=jnp.int32) // (D // block_count)
    spiked = pairing[row_block][:, None] == col_block[None, :]
    values = values * jnp.where(spiked, 3.0, 1.0)[None]
    return values.astype(jnp.bfloat16)


def weight_pair(key):
    first, second, third = jax.random.split(key, 3)
    kv_width = KV_HEADS * HEAD_DIM
    query_w = jnp.clip(jax.random.normal(first, (D, D), jnp.float32), -4.0, 4.0) / math.sqrt(D)
    value_w = jnp.clip(jax.random.normal(second, (D, kv_width), jnp.float32), -4.0, 4.0) / math.sqrt(D)
    key_w = jnp.clip(jax.random.normal(third, (D, kv_width), jnp.float32), -4.0, 4.0) / math.sqrt(D)
    return (query_w, jnp.concatenate([key_w, value_w], axis=1))


def draw_w_query(key, part):
    return weight_pair(jax.random.fold_in(key, 5))[0].astype(jnp.bfloat16)


def draw_w_keyval(key, part):
    return weight_pair(jax.random.fold_in(key, 5))[1].astype(jnp.bfloat16)


def levels(key, extent, pieces, smallest, high):
    def one(dim, shards_of):
        draws = jax.random.uniform(jax.random.fold_in(jax.random.fold_in(key, 6), dim), (shards_of,), jnp.float32, smallest / len(pieces), high / len(pieces))
        return jnp.repeat(jnp.exp(draws), extent[dim] // shards_of).reshape((-1,) + (1,) * (len(extent) - dim - 1))

    gain = one(*pieces[0])
    for cut in pieces[1:]:
        gain = gain * one(*cut)
    return gain


def profile(amount, total, reach, lean):
    loads = [(1 << 20) // math.isqrt(grade ** lean) + 1 for grade in range(2, amount + 1)]
    rest, holding = total - reach - (amount - 1), [1] * (amount - 1)
    while rest > 0:
        movable = [i for i in range(amount - 1) if holding[i] < reach]
        mass, left = sum([loads[i] for i in movable]), rest
        for i in movable:
            addition = min(reach - holding[i], max(1, left * loads[i] // mass), rest)
            holding[i] = holding[i] + addition
            rest = rest - addition
    return np.array([reach] + holding)


def uneven(key, number_of, total, bound, slope):
    if number_of == 2:
        one = jax.random.randint(key, (), max(1, total - bound), min(bound, total - 1) + 1)
        return jnp.stack([one, total - one])
    tallies = jnp.asarray(profile(number_of, total, bound, slope), jnp.int32)
    pairs = (number_of - 1) // 2
    source_of, sink = tallies[1:1 + 2 * pairs:2], tallies[2:2 + 2 * pairs:2]
    room = jnp.minimum(source_of - 1, bound - sink)
    moved = jax.random.randint(jax.random.fold_in(key, 1), (pairs,), 0, 1 << 20) % (room + 1)
    tallies = tallies.at[1:1 + 2 * pairs:2].set(source_of - moved).at[2:2 + 2 * pairs:2].set(sink + moved)
    return tallies[jax.random.permutation(jax.random.fold_in(key, 2), number_of)]


def gaussian(own_key, dims, width, limit, pieces=(), kind=jnp.bfloat16):
    drawn = width * jax.random.normal(own_key, dims, jnp.float32)
    if pieces:
        drawn = drawn * levels(own_key, dims, pieces, -0.22, 0.18)
    return jnp.clip(drawn, -limit, limit).astype(kind)


def setup_inputs(seed: int = 0) -> dict:
    arg_keys = jax.random.split(jax.random.key(seed), 6)
    tokens = draw_tokens(jax.random.fold_in(arg_keys[5], 71), 0)
    segments = jax.vmap(lambda own: jnp.searchsorted(jnp.cumsum(uneven(own, DOCS, SEQ, MOST, 1)), jnp.arange(SEQ), side="right"))(jax.random.split(arg_keys[1], GROUPS)).reshape((GROUPS, SEQ)).astype(jnp.int32)
    w_query = draw_w_query(jax.random.fold_in(arg_keys[5], 71), 0)
    w_keyval = draw_w_keyval(jax.random.fold_in(arg_keys[5], 71), 0)
    grad_context = gaussian(arg_keys[4], (GROUPS, SEQ, D), 1.0, 6.0, ((0, 4), (1, 8)))
    return dict(tokens=tokens, segments=segments, w_query=w_query, w_keyval=w_keyval, grad_context=grad_context)


def reference(tokens, segments, w_query, w_keyval, grad_context):
    halo_rows = WINDOW - BLOCK
    group_size = HEADS // KV_HEADS
    kv_width = KV_HEADS * HEAD_DIM
    score_scale = HEAD_DIM ** -0.5
    block_count = SEQ // BLOCK

    def per_group(weight_sum, items):
        hidden_in, doc_ids, grad_out = items
        queries = jnp.dot(hidden_in, w_query, preferred_element_type=jnp.float32).astype(jnp.bfloat16)
        keyval = jnp.dot(hidden_in, w_keyval, preferred_element_type=jnp.float32).astype(jnp.bfloat16)
        padded_kv = jnp.concatenate([jnp.zeros((halo_rows, KV_COLS), jnp.bfloat16), keyval], axis=0)
        padded_ids = jnp.concatenate([jnp.full((halo_rows,), -1, jnp.int32), doc_ids.astype(jnp.int32)], axis=0)

        def per_block(kv_grads, block_id):
            start = (block_id * BLOCK).astype(jnp.int32)
            query_blk = lax.dynamic_slice_in_dim(queries, start, BLOCK, 0).reshape(BLOCK, KV_HEADS, group_size, HEAD_DIM).astype(jnp.float32)
            out_blk = lax.dynamic_slice_in_dim(grad_out, start, BLOCK, 0).reshape(BLOCK, KV_HEADS, group_size, HEAD_DIM).astype(jnp.float32)
            kv_blk = lax.dynamic_slice_in_dim(padded_kv, start, WINDOW, 0)
            key_heads = kv_blk[:, :kv_width].reshape(WINDOW, KV_HEADS, HEAD_DIM).astype(jnp.float32)
            val_heads = kv_blk[:, kv_width:].reshape(WINDOW, KV_HEADS, HEAD_DIM).astype(jnp.float32)
            query_pos = start + jnp.arange(BLOCK, dtype=jnp.int32)
            key_pos = start - halo_rows + jnp.arange(WINDOW, dtype=jnp.int32)
            key_ids = lax.dynamic_slice_in_dim(padded_ids, start, WINDOW, 0)
            query_ids = lax.dynamic_slice_in_dim(doc_ids.astype(jnp.int32), start, BLOCK, 0)
            allowed = (key_pos[None, :] <= query_pos[:, None]) & (key_ids[None, :] == query_ids[:, None])
            scores = jnp.einsum("tgha,kga->ghtk", query_blk, key_heads) * score_scale
            masked = jnp.where(allowed[None, None], scores, -1e30)
            row_max = jnp.max(masked, axis=-1, keepdims=True)
            expo = jnp.exp(masked - row_max)
            attn_probs = expo / jnp.sum(expo, axis=-1, keepdims=True)
            probs_low = attn_probs.astype(jnp.bfloat16).astype(jnp.float32)
            ctx_heads = jnp.einsum("ghtk,kga->tgha", probs_low, val_heads).astype(jnp.bfloat16)
            row_delta = jnp.einsum("tgha,tgha->ght", out_blk, ctx_heads.astype(jnp.float32))
            grad_probs = jnp.einsum("tgha,kga->ghtk", out_blk, val_heads)
            grad_scores = (attn_probs * (grad_probs - row_delta[..., None]) * score_scale).astype(jnp.bfloat16).astype(jnp.float32)
            grad_q = jnp.einsum("ghtk,kga->tgha", grad_scores, key_heads).astype(jnp.bfloat16)
            grad_key = jnp.einsum("ghtk,tgha->kga", grad_scores, query_blk).reshape(WINDOW, kv_width)
            grad_val = jnp.einsum("ghtk,tgha->kga", probs_low, out_blk).reshape(WINDOW, kv_width)
            grad_kv = jnp.concatenate([grad_key, grad_val], axis=1)
            updated = lax.dynamic_slice_in_dim(kv_grads, start, WINDOW, 0) + grad_kv
            kv_grads = lax.dynamic_update_slice_in_dim(kv_grads, updated, start, 0)
            return kv_grads, (ctx_heads.reshape(BLOCK, D), grad_q.reshape(BLOCK, D))

        start_grads = jnp.zeros((halo_rows + SEQ, KV_COLS), jnp.float32)
        kv_grads, (ctx_blocks, grad_q_blocks) = lax.scan(per_block, start_grads, jnp.arange(block_count, dtype=jnp.int32))
        context = ctx_blocks.reshape(SEQ, D)
        grad_queries = grad_q_blocks.reshape(SEQ, D)
        grad_keyval = kv_grads[halo_rows:].astype(jnp.bfloat16)
        grad_in = jnp.dot(grad_queries, w_query.T, preferred_element_type=jnp.float32)
        grad_in = grad_in + jnp.dot(grad_keyval, w_keyval.T, preferred_element_type=jnp.float32)
        combined = jnp.concatenate([grad_queries, grad_keyval], axis=1)
        weight_sum = weight_sum + jnp.dot(hidden_in.T, combined, preferred_element_type=jnp.float32)
        return weight_sum, (context, grad_in.astype(jnp.bfloat16))

    start_sum = jnp.zeros((D, D + KV_COLS), jnp.float32)
    weight_sum, (contexts, grads_in) = lax.scan(per_group, start_sum, (tokens, segments, grad_context))
    weight_low = weight_sum.astype(jnp.bfloat16)
    return contexts, grads_in, weight_low[:, :D], weight_low[:, D:]
```

```python
import functools

import jax
import jax.numpy as jnp
from jax import lax
from jax.experimental import pallas as pl
from jax.experimental.pallas import tpu as pltpu
from jax.sharding import PartitionSpec as P

HEADS = 12
KV_HEADS = 2
HEAD_DIM = 128
WINDOW = 512
BLOCK = 128
HALO = WINDOW - BLOCK
GROUP = HEADS // KV_HEADS
COLUMNS = HEADS + 2 * KV_HEADS
SCALE = HEAD_DIM ** (-0.5)
MESH = pl.DeviceIdType.MESH
NT = (((1,), (1,)), ((), ()))
NN = (((1,), (0,)), ((), ()))
BF = jnp.bfloat16
F32 = jnp.float32


def dot(a, b, dims=NN):
    return lax.dot_general(a, b, dims, preferred_element_type=F32)


def layer_kernel(
    n_dp, n_ctx,
    tok_hbm, seg_ref, wq_hbm, wkv_hbm, do_hbm,
    ctx_ref, gi_ref, gwq_ref, gwkv_ref,
    tok, wq, wkv, do, tok_all, q, kv_all, ids_col, gkv, ghalo_out, ghalo_in, comb, comb_in,
    pair_out, pair_in, part_own, z_out, z_in, gath, gi_acc,
    load_s, tok_s, tok_r, halo_s, halo_r, gh_s, gh_r, comb_s, comb_r,
    pair_s, pair_r, z_s, z_r, fin_s, fin_r,
):
    n_z = n_ctx // 2
    slots = COLUMNS // n_dp
    tok_rows, model = tok.shape
    dp = lax.axis_index("dp")
    ctx = lax.axis_index("ctx")
    core = lax.rem(ctx, 2)
    mate = ctx + 1 - 2 * core
    other = lax.rem(ctx + 2 * core - 1 + n_ctx, n_ctx)
    level = ctx // 2
    rows = gwq_ref.shape[0]

    relayed = n_dp == 4

    def dp_peer(k):
        if relayed:
            return (dp + 1 - 2 * (dp % 2), dp + 2 - 4 * (dp // 2), 3 - dp)[k - 1]
        return lax.rem(dp + k, n_dp)

    def z_peer(k):
        return lax.rem(level + k, n_z)

    def remote(src, dst, send, recv, to_dp, to_ctx):
        return pltpu.make_async_remote_copy(
            src_ref=src, dst_ref=dst, send_sem=send, recv_sem=recv,
            device_id=(to_dp, to_ctx), device_id_type=MESH,
        )

    barrier = pltpu.get_barrier_semaphore()
    for k in range(1, n_dp):
        pl.semaphore_signal(barrier, inc=1, device_id=(dp_peer(k), ctx), device_id_type=MESH)
    for k in range(1, n_z):
        pl.semaphore_signal(
            barrier, inc=1, device_id=(dp, 2 * z_peer(k) + core), device_id_type=MESH
        )
    for to in (mate, other):
        pl.semaphore_signal(barrier, inc=1, device_id=(dp, to), device_id_type=MESH)

    loads = [
        pltpu.make_async_copy(src, dst, load_s.at[i])
        for i, (src, dst) in enumerate(
            [(tok_hbm, tok), (wkv_hbm, wkv), (wq_hbm, wq), (do_hbm, do)]
        )
    ]
    for copy in loads:
        copy.start()

    tile0 = ctx * (tok_rows // BLOCK) - HALO // BLOCK
    for t in range((HALO + tok_rows) // BLOCK):
        tile = tile0 + t
        start = pl.multiple_of(jnp.maximum(tile, 0) * BLOCK, BLOCK)
        row = seg_ref[0:1, pl.ds(start, BLOCK)]
        col = jnp.broadcast_to(row, (BLOCK, BLOCK)).T
        ids_col[t * BLOCK : (t + 1) * BLOCK, :] = jnp.where(tile < 0, -1, col)

    @pl.when(ctx < 1)
    def _():
        kv_all[BLOCK:HALO, :] = jnp.zeros((HALO - BLOCK, kv_all.shape[1]), BF)

    @pl.when(ctx < 2)
    def _():
        kv_all[0:BLOCK, :] = jnp.zeros((BLOCK, kv_all.shape[1]), BF)

    @pl.when(ctx >= n_ctx - 1)
    def _():
        ghalo_in[BLOCK:HALO, :] = jnp.zeros((HALO - BLOCK, kv_all.shape[1]), BF)

    @pl.when(ctx >= n_ctx - 2)
    def _():
        ghalo_in[0:BLOCK, :] = jnp.zeros((BLOCK, kv_all.shape[1]), BF)

    gkv[...] = jnp.zeros_like(gkv)
    loads[0].wait()
    for c in range(model // BLOCK):
        flipped = tok[:, c * BLOCK : (c + 1) * BLOCK].T
        at = c * BLOCK
        while at < (c + 1) * BLOCK:
            shard = at // rows
            upto = min((shard + 1) * rows, (c + 1) * BLOCK)
            low = (shard // 2) * rows + at - shard * rows
            tok_all[0, shard % 2, low : low + upto - at, :] = flipped[at - c * BLOCK : upto - c * BLOCK]
            at = upto

    loads[1].wait()
    kv_all[HALO:, :] = dot(tok[...], wkv[...]).astype(BF)
    pl.semaphore_wait(barrier, n_dp + n_z)

    def tok_copy(origin, slot, k, half):
        return remote(tok_all.at[origin, half], tok_all.at[slot, half], tok_s.at[slot - 1, half],
                      tok_r.at[slot - 1, half], dp_peer(k), ctx)

    tok_copies = {}
    for i in range(2):
        for k in range(1, 3 if relayed else n_dp):
            half = (i + k + 1) % 2
            tok_copies[k, half] = tok_copy(0, k, k, half)
            tok_copies[k, half].start()

    halo_copies = []
    for g in range(KV_HEADS):
        for i, part in enumerate((g, KV_HEADS + g)):
            c = slice(part * HEAD_DIM, (part + 1) * HEAD_DIM)
            one = remote(kv_all.at[HALO:, c], kv_all.at[BLOCK:HALO, c], halo_s.at[g, i, 0],
                         halo_r.at[g, i, 0], dp, lax.rem(ctx + 1, n_ctx))
            two = remote(kv_all.at[HALO + BLOCK :, c], kv_all.at[0:BLOCK, c], halo_s.at[g, i, 1],
                         halo_r.at[g, i, 1], dp, lax.rem(ctx + 2, n_ctx))
            halo_copies.append((one, two))

            @pl.when(ctx + 2 < n_ctx)
            def _():
                two.start()

            @pl.when(ctx + 1 < n_ctx)
            def _():
                one.start()

    loads[2].wait()
    for p in range(HEADS // 2):
        both = dot(tok[...], wq[:, 2 * p * HEAD_DIM : 2 * (p + 1) * HEAD_DIM]).astype(BF)
        q[2 * p] = both[:, :HEAD_DIM]
        q[2 * p + 1] = both[:, HEAD_DIM:]
    loads[3].wait()

    key_row = lax.broadcasted_iota(jnp.int32, (WINDOW, BLOCK), 0)
    query_col = lax.broadcasted_iota(jnp.int32, (WINDOW, BLOCK), 1)

    def attend(g, b):
        row0 = pl.multiple_of(b * BLOCK, BLOCK)
        kcol = slice(g * HEAD_DIM, (g + 1) * HEAD_DIM)
        vcol = slice((KV_HEADS + g) * HEAD_DIM, (KV_HEADS + g + 1) * HEAD_DIM)
        window = pl.ds(row0, WINDOW)
        block = pl.ds(row0, BLOCK)
        keys = kv_all[window, kcol]
        vals = kv_all[window, vcol]
        keys_t = keys.T
        vals_t = vals.T
        first = pl.multiple_of(ctx * tok_rows + b * BLOCK, BLOCK)
        same = ids_col[window, :] == seg_ref[0:1, pl.ds(first, BLOCK)]
        bias = jnp.where((key_row <= query_col + HALO) & same, 0.0, -1e30)
        bias = jnp.concatenate([bias, bias], axis=1)
        grad_key = jnp.zeros((WINDOW, HEAD_DIM), F32)
        grad_val = jnp.zeros((WINDOW, HEAD_DIM), F32)
        for pair in range(GROUP // 2):
            h = g * GROUP + 2 * pair
            cols = [slice((h + i) * HEAD_DIM, (h + i + 1) * HEAD_DIM) for i in range(2)]
            query = jnp.concatenate([q[h, block, :], q[h + 1, block, :]], axis=0)
            grad = jnp.concatenate([do[block, c] for c in cols], axis=0)
            masked = jnp.where(bias < 0.0, -1e30, dot(keys, query, NT) * SCALE)
            top = jnp.max(masked, axis=0, keepdims=True)
            expo = jnp.exp(masked - top)
            probs = expo * (1.0 / jnp.sum(expo, axis=0, keepdims=True))
            probs_low = probs.astype(BF)
            out_t = dot(vals_t, probs_low).astype(BF).astype(F32)
            delta = jnp.sum(out_t * grad.astype(F32).T, axis=0, keepdims=True)
            grad_scores = (probs * (dot(vals, grad, NT) - delta) * SCALE).astype(BF)
            grad_query = dot(keys_t, grad_scores).T.astype(BF)
            out = out_t.T.astype(BF)
            for i, c in enumerate(cols):
                ctx_ref[block, c] = out[i * BLOCK : (i + 1) * BLOCK]
                comb[h + i, block, :] = grad_query[i * BLOCK : (i + 1) * BLOCK]
            grad_key = grad_key + dot(grad_scores, query)
            grad_val = grad_val + dot(probs_low, grad)
        gkv[window, kcol] += grad_key
        gkv[window, vcol] += grad_val

    copies = {}

    def send_slot(s):
        for k in range(1, n_dp):
            copy = remote(comb.at[s * n_dp + dp_peer(k)], comb_in.at[s, k - 1],
                          comb_s.at[s, k - 1], comb_r.at[s, k - 1], dp_peer(k), ctx)
            copy.start()
            copies["comb", s, k] = copy

    def ready(s):
        last = (s + 1) * n_dp
        return 0 if last <= GROUP else 1 if last <= HEADS else 2

    gh_copies = []
    for g in range(KV_HEADS):
        for one, two in halo_copies[2 * g : 2 * g + 2]:
            @pl.when(ctx >= 1)
            def _():
                one.wait_recv()

            @pl.when(ctx >= 2)
            def _():
                two.wait_recv()

        @pl.loop(0, tok_rows // BLOCK)
        def _(b):
            attend(g, b)

        for i, part in enumerate((g, KV_HEADS + g)):
            c = slice(part * HEAD_DIM, (part + 1) * HEAD_DIM)
            ghalo_out[:, c] = gkv[0:HALO, c].astype(BF)
            one = remote(ghalo_out.at[BLOCK:HALO, c], ghalo_in.at[BLOCK:HALO, c],
                         gh_s.at[g, i, 0], gh_r.at[g, i, 0], dp, lax.rem(ctx + n_ctx - 1, n_ctx))
            two = remote(ghalo_out.at[0:BLOCK, c], ghalo_in.at[0:BLOCK, c],
                         gh_s.at[g, i, 1], gh_r.at[g, i, 1], dp, lax.rem(ctx + n_ctx - 2, n_ctx))
            gh_copies.append((one, two))

            @pl.when(ctx >= 2)
            def _():
                two.start()

            @pl.when(ctx >= 1)
            def _():
                one.start()

        if g == 0 and relayed:
            tok_copies[1, 0].wait_recv()
            tok_copies[3, 0] = tok_copy(1, 3, 2, 0)
            tok_copies[3, 0].start()
            tok_copies[2, 1].wait_recv()
            tok_copies[3, 1] = tok_copy(2, 3, 1, 1)
            tok_copies[3, 1].start()

        for s in range(slots):
            if ready(s) == g:
                send_slot(s)

    def finish_keyval():
        for one, two in gh_copies:
            @pl.when(ctx + 1 < n_ctx)
            def _():
                one.wait_recv()

            @pl.when(ctx + 2 < n_ctx)
            def _():
                two.wait_recv()

        for part in range(2 * KV_HEADS):
            c = slice(part * HEAD_DIM, (part + 1) * HEAD_DIM)
            near = gkv[HALO:, c] + ghalo_in[BLOCK:HALO, c].astype(F32)
            comb[HEADS + part, 0:BLOCK, :] = near[0:BLOCK].astype(BF)
            comb[HEADS + part, BLOCK:, :] = (near[BLOCK:] + ghalo_in[0:BLOCK, c].astype(F32)).astype(BF)
        for s in range(slots):
            if ready(s) == 2:
                send_slot(s)

    def partial(s, parity):
        total = dot(tok_all[0, parity], comb[s * n_dp + dp])
        for k in range(1, n_dp):
            total = total + dot(tok_all[k, parity], comb_in[s, k - 1])
        return total

    def multiply(s):
        for k in range(1, n_dp):
            copies["comb", s, k].wait_recv()
        pair_out[s] = partial(s, 1 - core).astype(BF)
        copy = remote(pair_out.at[s], pair_in.at[s], pair_s.at[s], pair_r.at[s], dp, mate)
        copy.start()
        copies["pair", s] = copy
        part_own[s] = partial(s, core)

    def spread(s):
        copies["pair", s].wait_recv()
        z_out[s] = (part_own[s] + pair_in[s].astype(F32)).astype(BF)
        for k in range(1, n_z):
            piece = pl.ds(pl.multiple_of(z_peer(k) * rows, 16), rows)
            copy = remote(z_out.at[s, piece], z_in.at[s, k - 1], z_s.at[s, k - 1], z_r.at[s, k - 1],
                          dp, 2 * z_peer(k) + core)
            copy.start()
            copies["z", s, k] = copy

    def collect(s):
        mine = pl.ds(pl.multiple_of(level * rows, 16), rows)
        total = part_own[s, mine] + pair_in[s, mine].astype(F32)
        for k in range(1, n_z):
            copies["z", s, k].wait_recv()
            total = total + z_in[s, k - 1].astype(F32)
        spot = s * n_dp + dp
        gath[spot] = total.astype(BF)
        for k in range(1, n_dp):
            copy = remote(gath.at[spot], gath.at[spot], fin_s.at[s, k - 1], fin_r.at[s, k - 1],
                          dp_peer(k), ctx)
            copy.start()
            copies["fin", s, k] = copy

    def grad_in(low, high, last):
        @pl.loop(0, model // 256)
        def _(r):
            part = pl.ds(pl.multiple_of(r * 256, 256), 256)
            total = gi_acc[r] if last else jnp.zeros((256, tok_rows), F32)
            for p in range(low, high, 2):
                pairs = jnp.concatenate([comb[p], comb[p + 1]], axis=1)
                if p < HEADS:
                    weight = wq[part, p * HEAD_DIM : (p + 2) * HEAD_DIM]
                else:
                    weight = wkv[part, (p - HEADS) * HEAD_DIM : (p + 2 - HEADS) * HEAD_DIM]
                total = total + dot(weight, pairs, NT)
            if last:
                gi_ref[:, part] = total.T.astype(BF)
            else:
                gi_acc[r] = total

    early = [s for s in range(slots) if ready(s) < 2]
    late = [s for s in range(slots) if ready(s) == 2]
    order = early + late
    grad_in(0, HEADS, False)
    finish_keyval()
    grad_in(HEADS, COLUMNS, True)
    for (k, half), copy in tok_copies.items():
        if not relayed or (k, half) not in ((1, 0), (2, 1)):
            copy.wait_recv()
    for i in range(slots + 1):
        if i < slots:
            multiply(order[i])
        if i > 0:
            spread(order[i - 1])
    for s in order:
        collect(s)
    for name, copy in copies.items():
        if name[0] == "fin":
            copy.wait_recv()
    for j in range(COLUMNS):
        if j < HEADS:
            gwq_ref[:, j * HEAD_DIM : (j + 1) * HEAD_DIM] = gath[j]
        else:
            gwkv_ref[:, (j - HEADS) * HEAD_DIM : (j - HEADS + 1) * HEAD_DIM] = gath[j]
    for copy in list(copies.values()) + list(tok_copies.values()):
        copy.wait_send()
    for one, two in halo_copies:
        @pl.when(ctx + 1 < n_ctx)
        def _():
            one.wait_send()

        @pl.when(ctx + 2 < n_ctx)
        def _():
            two.wait_send()

    for one, two in gh_copies:
        @pl.when(ctx >= 1)
        def _():
            one.wait_send()

        @pl.when(ctx >= 2)
        def _():
            two.wait_send()


def square_kernel(
    n_ctx,
    tok_hbm, seg_ref, wq_hbm, wkv_hbm, do_hbm,
    ctx_ref, gi_ref, gwq_ref, gwkv_ref,
    tok, wq, wkv, do, tok_own, tok_in, q, kv_all, flip_all, ids_col, bias_ref, gkv, ghalo_out, ghalo_in,
    comb, comb_in, pair_out, pair_in, part_own, half_out, half_in, z_out, z_in, gath, gi_acc,
    load_s, tok_s, tok_r, halo_s, halo_r, gh_s, gh_r, comb_s, comb_r,
    pair_s, pair_r, half_s, half_r, z_s, z_r, fin_s, fin_r,
):
    n_z = n_ctx // 2
    n_h = n_z // 2
    tok_rows, model = tok.shape
    blocks = tok_rows // BLOCK
    dp = lax.axis_index("dp")
    ctx = lax.axis_index("ctx")
    core = lax.rem(ctx, 2)
    mate = ctx + 1 - 2 * core
    other = lax.rem(ctx + 2 * core - 1 + n_ctx, n_ctx)
    level = ctx // 2
    rows = gwq_ref.shape[0]
    part = rows // 2
    fast, slow = dp % 2, dp // 2
    place = ((fast, slow), (slow, fast))
    peers = (dp + 1 - 2 * fast, dp + 2 - 4 * slow, 3 - dp)
    top_half = level < n_h
    own_first = jnp.where(top_half, fast, slow)
    own_second = jnp.where(top_half, slow, fast)

    slots = [(0, 2), (4, 2), (8, 2), (HEADS, 1), (HEADS + 2, 1)]
    offsets = [0, 2, 4, 6, 7]

    def z_peer(k):
        return lax.rem(level + k, n_z)

    def remote(src, dst, send, recv, to_dp, to_ctx):
        return pltpu.make_async_remote_copy(
            src_ref=src, dst_ref=dst, send_sem=send, recv_sem=recv,
            device_id=(to_dp, to_ctx), device_id_type=MESH,
        )

    barrier = pltpu.get_barrier_semaphore()
    for peer in peers:
        pl.semaphore_signal(barrier, inc=1, device_id=(peer, ctx), device_id_type=MESH)
    for k in range(1, n_z):
        pl.semaphore_signal(
            barrier, inc=1, device_id=(dp, 2 * z_peer(k) + core), device_id_type=MESH
        )
    for to in (mate, other):
        pl.semaphore_signal(barrier, inc=1, device_id=(dp, to), device_id_type=MESH)

    loads = [
        pltpu.make_async_copy(src, dst, load_s.at[i])
        for i, (src, dst) in enumerate(
            [(tok_hbm, tok), (wkv_hbm, wkv), (wq_hbm, wq), (do_hbm, do)]
        )
    ]
    for copy in loads:
        copy.start()

    tile0 = ctx * blocks - HALO // BLOCK
    for t in range(HALO // BLOCK + blocks):
        tile = tile0 + t
        start = pl.multiple_of(jnp.maximum(tile, 0) * BLOCK, BLOCK)
        row = seg_ref[0:1, pl.ds(start, BLOCK)]
        col = jnp.broadcast_to(row, (BLOCK, BLOCK)).T
        ids_col[t * BLOCK : (t + 1) * BLOCK, :] = jnp.where(tile < 0, -1, col)
    key_row = lax.broadcasted_iota(jnp.int32, (WINDOW, BLOCK), 0)
    query_col = lax.broadcasted_iota(jnp.int32, (WINDOW, BLOCK), 1)
    for b in range(blocks):
        first = pl.multiple_of(ctx * tok_rows + b * BLOCK, BLOCK)
        same = ids_col[b * BLOCK : b * BLOCK + WINDOW, :] == seg_ref[0:1, pl.ds(first, BLOCK)]
        bias_ref[b] = jnp.where((key_row <= query_col + HALO) & same, 0.0, -1e30)

    @pl.when(ctx < 1)
    def _():
        kv_all[BLOCK:HALO, :] = jnp.zeros((HALO - BLOCK, kv_all.shape[1]), BF)

    @pl.when(ctx < 2)
    def _():
        kv_all[0:BLOCK, :] = jnp.zeros((BLOCK, kv_all.shape[1]), BF)

    @pl.when(ctx >= n_ctx - 1)
    def _():
        ghalo_in[BLOCK:HALO, :] = jnp.zeros((HALO - BLOCK, kv_all.shape[1]), BF)

    @pl.when(ctx >= n_ctx - 2)
    def _():
        ghalo_in[0:BLOCK, :] = jnp.zeros((BLOCK, kv_all.shape[1]), BF)

    gkv[...] = jnp.zeros_like(gkv)
    loads[0].wait()
    loads[1].wait()
    kv_all[HALO:, :] = dot(tok[...], wkv[...]).astype(BF)
    for c in range(model // BLOCK):
        flipped = tok[:, c * BLOCK : (c + 1) * BLOCK].T
        at = c * BLOCK
        while at < (c + 1) * BLOCK:
            shard = at // rows
            upto = min((shard + 1) * rows, (c + 1) * BLOCK)
            z = shard // 2
            low = (z % n_h) * rows + at - shard * rows
            tok_own[z // n_h, shard % 2, low : low + upto - at, :] = flipped[at - c * BLOCK : upto - c * BLOCK]
            at = upto
    pl.semaphore_wait(barrier, 4 + n_z)

    halo_copies = []
    for g in range(KV_HEADS):
        for i, piece in enumerate((g, KV_HEADS + g)):
            c = slice(piece * HEAD_DIM, (piece + 1) * HEAD_DIM)
            one = remote(kv_all.at[HALO:, c], kv_all.at[BLOCK:HALO, c], halo_s.at[g, i, 0],
                         halo_r.at[g, i, 0], dp, lax.rem(ctx + 1, n_ctx))
            two = remote(kv_all.at[HALO + BLOCK :, c], kv_all.at[0:BLOCK, c], halo_s.at[g, i, 1],
                         halo_r.at[g, i, 1], dp, lax.rem(ctx + 2, n_ctx))
            halo_copies.append((one, two))

            @pl.when(ctx + 2 < n_ctx)
            def _():
                two.start()

            @pl.when(ctx + 1 < n_ctx)
            def _():
                one.start()

    tok_copies = [
        remote(tok_own.at[r], tok_in.at[r], tok_s.at[r], tok_r.at[r], peers[r], ctx) for r in range(2)
    ]
    for copy in tok_copies:
        copy.start()

    loads[2].wait()
    for p in range(HEADS // 2):
        both = dot(tok[...], wq[:, 2 * p * HEAD_DIM : 2 * (p + 1) * HEAD_DIM]).astype(BF)
        q[2 * p] = both[:, :HEAD_DIM]
        q[2 * p + 1] = both[:, HEAD_DIM:]
    loads[3].wait()

    def columns(g):
        return [slice(j * HEAD_DIM, (j + 1) * HEAD_DIM) for j in (g, KV_HEADS + g)]

    def attend(g, p, b):
        row0 = b * BLOCK
        kcol, vcol = columns(g)
        window = slice(row0, row0 + WINDOW)
        block = slice(row0, row0 + BLOCK)
        keys = kv_all[window, kcol]
        vals = kv_all[window, vcol]
        keys_t = flip_all[0, :, window]
        vals_t = flip_all[1, :, window]
        bias = bias_ref[b]
        bias = jnp.concatenate([bias, bias], axis=1)
        h = g * GROUP + 2 * p
        cols = [slice((h + i) * HEAD_DIM, (h + i + 1) * HEAD_DIM) for i in range(2)]
        query = jnp.concatenate([q[h, block, :], q[h + 1, block, :]], axis=0)
        grad = jnp.concatenate([do[block, c] for c in cols], axis=0)
        masked = dot(keys, query, NT) * SCALE + bias
        top = jnp.max(masked, axis=0, keepdims=True)
        expo = jnp.exp(masked - top)
        probs = expo * (1.0 / jnp.sum(expo, axis=0, keepdims=True))
        probs_low = probs.astype(BF)
        out_t = dot(vals_t, probs_low).astype(BF).astype(F32)
        delta = jnp.sum(out_t * grad.astype(F32).T, axis=0, keepdims=True)
        grad_scores = (probs * (dot(vals, grad, NT) - delta) * SCALE).astype(BF)
        grad_query = dot(keys_t, grad_scores).T.astype(BF)
        out = out_t.T.astype(BF)
        for i, c in enumerate(cols):
            ctx_ref[block, c] = out[i * BLOCK : (i + 1) * BLOCK]
            comb[h + i, block, :] = grad_query[i * BLOCK : (i + 1) * BLOCK]
        gkv[window, kcol] += dot(grad_scores, query)
        gkv[window, vcol] += dot(probs_low, grad)

    copies = {}

    def start_group(g):
        for one, two in halo_copies[2 * g : 2 * g + 2]:
            @pl.when(ctx >= 1)
            def _():
                one.wait_recv()

            @pl.when(ctx >= 2)
            def _():
                two.wait_recv()

        for i, c in enumerate(columns(g)):
            flip_all[i] = kv_all[:, c].T

    gh_copies = {}

    def send_halo(g):
        gh_copies[g] = []
        for i, c in enumerate(columns(g)):
            ghalo_out[:, c] = gkv[0:HALO, c].astype(BF)
            one = remote(ghalo_out.at[BLOCK:HALO, c], ghalo_in.at[BLOCK:HALO, c],
                         gh_s.at[g, i, 0], gh_r.at[g, i, 0], dp, lax.rem(ctx + n_ctx - 1, n_ctx))
            two = remote(ghalo_out.at[0:BLOCK, c], ghalo_in.at[0:BLOCK, c],
                         gh_s.at[g, i, 1], gh_r.at[g, i, 1], dp, lax.rem(ctx + n_ctx - 2, n_ctx))
            gh_copies[g].append((one, two))

            @pl.when(ctx >= 2)
            def _():
                two.start()

            @pl.when(ctx >= 1)
            def _():
                one.start()

    def finish_keyval(g):
        for one, two in gh_copies[g]:
            @pl.when(ctx + 1 < n_ctx)
            def _():
                one.wait_recv()

            @pl.when(ctx + 2 < n_ctx)
            def _():
                two.wait_recv()

        for i, c in enumerate(columns(g)):
            near = gkv[HALO:, c] + ghalo_in[BLOCK:HALO, c].astype(F32)
            at = HEADS + 2 * g + i
            comb[at, 0:BLOCK, :] = near[0:BLOCK].astype(BF)
            comb[at, BLOCK:, :] = (near[BLOCK:] + ghalo_in[0:BLOCK, c].astype(F32)).astype(BF)

    def send_slot(s):
        (low, width), at = slots[s], offsets[s]
        for r in range(2):
            theirs = pl.ds(low + width * (1 - place[r][0]), width)
            copy = remote(comb.at[theirs], comb_in.at[r, at : at + width], comb_s.at[s, r], comb_r.at[s, r],
                          peers[r], ctx)
            copy.start()
            copies["comb", s, r] = copy

    def multiply(s):
        (low, width), at = slots[s], offsets[s]
        for r in range(2):
            copies["comb", s, r].wait_recv()

        def product(r, parity):
            mine = [comb[low + width * place[r][0] + i] for i in range(width)]
            theirs = [comb_in[r, at + i] for i in range(width)]
            total = dot(tok_own[r, parity], jnp.concatenate(mine, axis=1))
            total = total + dot(tok_in[r, parity], jnp.concatenate(theirs, axis=1))
            return [total[:, i * HEAD_DIM : (i + 1) * HEAD_DIM] for i in range(width)]

        for r in range(2):
            for i, piece in enumerate(product(r, 1 - core)):
                pair_out[at + i, r] = piece.astype(BF)
        copy = remote(pair_out.at[at : at + width], pair_in.at[at : at + width], pair_s.at[s], pair_r.at[s],
                      dp, mate)
        copy.start()
        copies["pair", s] = copy
        for r in range(2):
            for i, piece in enumerate(product(r, core)):
                part_own[at + i, r] = piece

    def halve(s):
        (_, width), at = slots[s], offsets[s]
        copies["pair", s].wait_recv()
        for r in range(2):
            for i in range(at, at + width):
                for z in range(n_h):
                    away = pl.ds(pl.multiple_of(z * rows + (1 - place[r][1]) * part, 16), part)
                    total = part_own[i, r, away] + pair_in[i, r, away].astype(F32)
                    half_out[r, i, z] = total.astype(BF)
            copy = remote(half_out.at[r, at : at + width], half_in.at[r, at : at + width], half_s.at[s, r],
                          half_r.at[s, r], peers[1 - r], ctx)
            copy.start()
            copies["half", s, r] = copy

    def spread(s):
        (_, width), at = slots[s], offsets[s]
        for r in range(2):
            copies["half", s, r].wait_recv()
        for r in range(2):
            for z in range(n_h):
                for i in range(at, at + width):
                    here = pl.ds(pl.multiple_of(z * rows + place[r][1] * part, 16), part)
                    total = part_own[i, r, here] + pair_in[i, r, here].astype(F32)
                    total = total + half_in[r, i, z].astype(F32)
                    z_out[r * n_h + z, i] = total.astype(BF)
        for k in range(1, n_z):
            copy = remote(z_out.at[z_peer(k), at : at + width], z_in.at[k - 1, at : at + width],
                          z_s.at[s, k - 1], z_r.at[s, k - 1], dp, 2 * z_peer(k) + core)
            copy.start()
            copies["z", s, k] = copy

    def collect(s):
        (low, width), at = slots[s], offsets[s]
        r, z = level // n_h, lax.rem(level, n_h)
        here = pl.ds(pl.multiple_of(z * rows + own_second * part, 16), part)
        totals = [
            part_own[i, r, here] + pair_in[i, r, here].astype(F32) + half_in[r, i, z].astype(F32)
            for i in range(at, at + width)
        ]
        for k in range(1, n_z):
            copies["z", s, k].wait_recv()
            totals = [total + z_in[k - 1, at + i].astype(F32) for i, total in enumerate(totals)]
        spot = pl.ds(pl.multiple_of(own_second * part, 16), part)
        for i, total in enumerate(totals):
            gath[low + width * own_first + i, spot, :] = total.astype(BF)
        held = gath.at[pl.ds(low + width * own_first, width), spot, :]
        for k, peer in enumerate(peers):
            copy = remote(held, held, fin_s.at[s, k], fin_r.at[s, k], peer, ctx)
            copy.start()
            copies["fin", s, k] = copy

    def grad_in(r, low, high, last):
        rows_in = slice(r * 256, (r + 1) * 256)
        total = gi_acc[r] if low else jnp.zeros((256, tok_rows), F32)
        for p in range(low, high, 2):
            pairs = jnp.concatenate([comb[p], comb[p + 1]], axis=1)
            if p < HEADS:
                weight = wq[rows_in, p * HEAD_DIM : (p + 2) * HEAD_DIM]
            else:
                weight = jnp.concatenate([wkv[rows_in, c] for c in columns((p - HEADS) // 2)], axis=1)
            total = total + dot(weight, pairs, NT)
        if last:
            gi_ref[:, rows_in] = total.T.astype(BF)
        else:
            gi_acc[r] = total

    chunks = model // 256
    start_group(0)
    for p in range(GROUP // 2):
        for b in reversed(range(blocks)):
            attend(0, p, b)
        if p == 1:
            send_slot(0)
    send_halo(0)
    start_group(1)
    for p in range(GROUP // 2):
        for b in reversed(range(blocks)):
            attend(1, p, b)
        if p == 0:
            send_slot(1)
            for copy in tok_copies:
                copy.wait_recv()
            multiply(0)
        if p == 1:
            finish_keyval(0)
            send_slot(3)
            halve(0)
    send_halo(1)
    send_slot(2)
    multiply(1)
    spread(0)
    halve(1)
    multiply(3)
    grad_in(0, 0, HEADS, False)
    halve(3)
    multiply(2)
    collect(0)
    spread(1)
    halve(2)
    finish_keyval(1)
    send_slot(4)
    spread(3)
    grad_in(1, 0, HEADS, False)
    spread(2)
    collect(1)
    grad_in(2, 0, HEADS, False)
    multiply(4)
    collect(3)
    halve(4)
    grad_in(3, 0, HEADS, False)
    collect(2)
    grad_in(4, 0, HEADS, False)
    spread(4)
    grad_in(5, 0, HEADS, False)
    for r in range(chunks):
        grad_in(r, HEADS, COLUMNS, True)
    collect(4)
    for name, copy in copies.items():
        if name[0] == "fin":
            copy.wait_recv()
    for j in range(COLUMNS):
        if j < HEADS:
            gwq_ref[:, j * HEAD_DIM : (j + 1) * HEAD_DIM] = gath[j]
        else:
            at = KV_HEADS * ((j - HEADS) % 2) + (j - HEADS) // 2
            gwkv_ref[:, at * HEAD_DIM : (at + 1) * HEAD_DIM] = gath[j]
    for copy in list(copies.values()) + tok_copies:
        copy.wait_send()
    for one, two in halo_copies:
        @pl.when(ctx + 1 < n_ctx)
        def _():
            one.wait_send()

        @pl.when(ctx + 2 < n_ctx)
        def _():
            two.wait_send()

    for g in range(KV_HEADS):
        for one, two in gh_copies[g]:
            @pl.when(ctx >= 1)
            def _():
                one.wait_send()

            @pl.when(ctx >= 2)
            def _():
                two.wait_send()


def copy_kernel(*refs):
    count = (len(refs) - 2) // 3
    sources, targets, held = refs[:count], refs[count : 2 * count], refs[2 * count : 3 * count]
    in_s, out_s = refs[-2:]
    arrive = [pltpu.make_async_copy(sources[i], held[i], in_s.at[i]) for i in range(count)]
    leave = [pltpu.make_async_copy(held[i], targets[i], out_s.at[i]) for i in range(count)]
    for copy in arrive:
        copy.start()
    for i in range(count):
        arrive[i].wait()
        leave[i].start()
    for copy in leave:
        copy.wait()


def copied(arrays):
    hbm = pl.BlockSpec(memory_space=pl.ANY)
    return pl.pallas_call(
        copy_kernel,
        out_shape=tuple(jax.ShapeDtypeStruct(a.shape, a.dtype) for a in arrays),
        in_specs=[hbm] * len(arrays),
        out_specs=(hbm,) * len(arrays),
        scratch_shapes=[pltpu.VMEM(a.shape, a.dtype) for a in arrays]
        + [pltpu.SemaphoreType.DMA((len(arrays),))] * 2,
        name="results",
    )(*arrays)


def square_scratch(n_ctx, tok_rows, model, kv_cols):
    n_z = n_ctx // 2
    n_h = n_z // 2
    rows = model // n_ctx
    part = rows // 2
    keys = HALO + tok_rows
    held = COLUMNS // 2
    dma = pltpu.SemaphoreType.DMA
    return [
        pltpu.VMEM((tok_rows, model), BF),
        pltpu.VMEM((model, model), BF),
        pltpu.VMEM((model, kv_cols), BF),
        pltpu.VMEM((tok_rows, model), BF),
        pltpu.VMEM((2, 2, n_h * rows, tok_rows), BF),
        pltpu.VMEM((2, 2, n_h * rows, tok_rows), BF),
        pltpu.VMEM((HEADS, tok_rows, HEAD_DIM), BF),
        pltpu.VMEM((keys, kv_cols), BF),
        pltpu.VMEM((2, HEAD_DIM, keys), BF),
        pltpu.VMEM((keys, BLOCK), jnp.int32),
        pltpu.VMEM((tok_rows // BLOCK, WINDOW, BLOCK), F32),
        pltpu.VMEM((keys, kv_cols), F32),
        pltpu.VMEM((HALO, kv_cols), BF),
        pltpu.VMEM((HALO, kv_cols), BF),
        pltpu.VMEM((COLUMNS, tok_rows, HEAD_DIM), BF),
        pltpu.VMEM((2, held, tok_rows, HEAD_DIM), BF),
        pltpu.VMEM((held, 2, n_h * rows, HEAD_DIM), BF),
        pltpu.VMEM((held, 2, n_h * rows, HEAD_DIM), BF),
        pltpu.VMEM((held, 2, n_h * rows, HEAD_DIM), F32),
        pltpu.VMEM((2, held, n_h, part, HEAD_DIM), BF),
        pltpu.VMEM((2, held, n_h, part, HEAD_DIM), BF),
        pltpu.VMEM((n_z, held, part, HEAD_DIM), BF),
        pltpu.VMEM((n_z - 1, held, part, HEAD_DIM), BF),
        pltpu.VMEM((COLUMNS, rows, HEAD_DIM), BF),
        pltpu.VMEM((model // 256, 256, tok_rows), F32),
        dma((4,)),
        dma((2,)), dma((2,)),
        dma((KV_HEADS, 2, 2)), dma((KV_HEADS, 2, 2)),
        dma((KV_HEADS, 2, 2)), dma((KV_HEADS, 2, 2)),
        dma((5, 2)), dma((5, 2)),
        dma((5,)), dma((5,)),
        dma((5, 2)), dma((5, 2)),
        dma((5, n_z - 1)), dma((5, n_z - 1)),
        dma((5, 3)), dma((5, 3)),
    ]


def shards(tokens, segments, w_query, w_keyval, grad_context):
    hidden_in = tokens[0]
    tok_rows, model = hidden_in.shape
    kv_cols = w_keyval.shape[1]
    n_ctx = lax.axis_size("ctx")
    n_dp = lax.axis_size("dp")
    n_z = n_ctx // 2
    rows = model // n_ctx
    slots = COLUMNS // n_dp
    half = n_z * rows
    square = n_dp == 4 and n_ctx % 4 == 0 and rows % 32 == 0
    keys = HALO + tok_rows
    vmem = pl.BlockSpec(memory_space=pltpu.VMEM)
    hbm = pl.BlockSpec(memory_space=pl.ANY)
    dma = pltpu.SemaphoreType.DMA
    results = pl.pallas_call(
        functools.partial(square_kernel, n_ctx) if square else functools.partial(layer_kernel, n_dp, n_ctx),
        out_shape=(
            jax.ShapeDtypeStruct((tok_rows, model), BF),
            jax.ShapeDtypeStruct((tok_rows, model), BF),
            jax.ShapeDtypeStruct((rows, model), BF),
            jax.ShapeDtypeStruct((rows, kv_cols), BF),
        ),
        in_specs=[hbm, vmem, hbm, hbm, hbm],
        out_specs=(vmem,) * 4,
        scratch_shapes=square_scratch(n_ctx, tok_rows, model, kv_cols) if square else [
            pltpu.VMEM((tok_rows, model), BF),
            pltpu.VMEM((model, model), BF),
            pltpu.VMEM((model, kv_cols), BF),
            pltpu.VMEM((tok_rows, model), BF),
            pltpu.VMEM((n_dp, 2, half, tok_rows), BF),
            pltpu.VMEM((HEADS, tok_rows, HEAD_DIM), BF),
            pltpu.VMEM((keys, kv_cols), BF),
            pltpu.VMEM((keys, BLOCK), jnp.int32),
            pltpu.VMEM((keys, kv_cols), F32),
            pltpu.VMEM((HALO, kv_cols), BF),
            pltpu.VMEM((HALO, kv_cols), BF),
            pltpu.VMEM((COLUMNS, tok_rows, HEAD_DIM), BF),
            pltpu.VMEM((slots, n_dp - 1, tok_rows, HEAD_DIM), BF),
            pltpu.VMEM((slots, half, HEAD_DIM), BF),
            pltpu.VMEM((slots, half, HEAD_DIM), BF),
            pltpu.VMEM((slots, half, HEAD_DIM), F32),
            pltpu.VMEM((slots, half, HEAD_DIM), BF),
            pltpu.VMEM((slots, n_z - 1, rows, HEAD_DIM), BF),
            pltpu.VMEM((COLUMNS, rows, HEAD_DIM), BF),
            pltpu.VMEM((model // 256, 256, tok_rows), F32),
            dma((4,)),
            dma((n_dp - 1, 2)), dma((n_dp - 1, 2)),
            dma((KV_HEADS, 2, 2)), dma((KV_HEADS, 2, 2)),
            dma((KV_HEADS, 2, 2)), dma((KV_HEADS, 2, 2)),
            dma((slots, n_dp - 1)), dma((slots, n_dp - 1)),
            dma((slots,)), dma((slots,)),
            dma((slots, n_z - 1)), dma((slots, n_z - 1)),
            dma((slots, n_dp - 1)), dma((slots, n_dp - 1)),
        ],
        compiler_params=pltpu.CompilerParams(
            collective_id=0, has_side_effects=True, vmem_limit_bytes=60 * 1024 * 1024
        ),
        name="layer",
    )(hidden_in, segments, w_query, w_keyval, grad_context[0])
    context, grad_in, grad_wq, grad_wkv = copied(results)
    return context[None], grad_in[None], grad_wq, grad_wkv


def solution(mesh):
    placed = (P("dp", "ctx", None), P("dp", None), P(), P(), P("dp", "ctx", None))
    return jax.shard_map(
        shards,
        mesh=mesh,
        in_specs=placed,
        out_specs=(P("dp", "ctx", None), P("dp", "ctx", None), P("ctx", None), P("ctx", None)),
        check_vma=False,
    )
```

```python
import functools

import jax
import jax.numpy as jnp
from jax import lax
from jax.experimental import pallas as pl
from jax.experimental.pallas import tpu as pltpu
from jax.sharding import PartitionSpec as P

HEADS = 12
KV_HEADS = 2
HEAD_DIM = 128
WINDOW = 512
BLOCK = 128
HALO = WINDOW - BLOCK
GROUP = HEADS // KV_HEADS
COLUMNS = HEADS + 2 * KV_HEADS
SCALE = HEAD_DIM ** (-0.5)
MESH = pl.DeviceIdType.MESH
NT = (((1,), (1,)), ((), ()))
NN = (((1,), (0,)), ((), ()))
BF = jnp.bfloat16
F32 = jnp.float32


def dot(a, b, dims=NN):
    return lax.dot_general(a, b, dims, preferred_element_type=F32)


def layer_kernel(
    n_dp, n_ctx,
    tok_hbm, seg_ref, wq_hbm, wkv_hbm, do_hbm,
    ctx_ref, gi_ref, gwq_ref, gwkv_ref,
    tok, wq, wkv, do, tok_all, q, kv_all, ids_col, gkv, ghalo_out, ghalo_in, comb, comb_in,
    pair_out, pair_in, part_own, z_out, z_in, gath, gi_acc,
    load_s, tok_s, tok_r, halo_s, halo_r, gh_s, gh_r, comb_s, comb_r,
    pair_s, pair_r, z_s, z_r, fin_s, fin_r,
):
    n_z = n_ctx // 2
    slots = COLUMNS // n_dp
    tok_rows, model = tok.shape
    dp = lax.axis_index("dp")
    ctx = lax.axis_index("ctx")
    core = lax.rem(ctx, 2)
    mate = ctx + 1 - 2 * core
    other = lax.rem(ctx + 2 * core - 1 + n_ctx, n_ctx)
    level = ctx // 2
    rows = gwq_ref.shape[0]

    relayed = n_dp == 4

    def dp_peer(k):
        if relayed:
            return (dp + 1 - 2 * (dp % 2), dp + 2 - 4 * (dp // 2), 3 - dp)[k - 1]
        return lax.rem(dp + k, n_dp)

    def z_peer(k):
        return lax.rem(level + k, n_z)

    def remote(src, dst, send, recv, to_dp, to_ctx):
        return pltpu.make_async_remote_copy(
            src_ref=src, dst_ref=dst, send_sem=send, recv_sem=recv,
            device_id=(to_dp, to_ctx), device_id_type=MESH,
        )

    barrier = pltpu.get_barrier_semaphore()
    for k in range(1, n_dp):
        pl.semaphore_signal(barrier, inc=1, device_id=(dp_peer(k), ctx), device_id_type=MESH)
    for k in range(1, n_z):
        pl.semaphore_signal(
            barrier, inc=1, device_id=(dp, 2 * z_peer(k) + core), device_id_type=MESH
        )
    for to in (mate, other):
        pl.semaphore_signal(barrier, inc=1, device_id=(dp, to), device_id_type=MESH)

    loads = [
        pltpu.make_async_copy(src, dst, load_s.at[i])
        for i, (src, dst) in enumerate(
            [(tok_hbm, tok), (wkv_hbm, wkv), (wq_hbm, wq), (do_hbm, do)]
        )
    ]
    for copy in loads:
        copy.start()

    tile0 = ctx * (tok_rows // BLOCK) - HALO // BLOCK
    for t in range((HALO + tok_rows) // BLOCK):
        tile = tile0 + t
        start = pl.multiple_of(jnp.maximum(tile, 0) * BLOCK, BLOCK)
        row = seg_ref[0:1, pl.ds(start, BLOCK)]
        col = jnp.broadcast_to(row, (BLOCK, BLOCK)).T
        ids_col[t * BLOCK : (t + 1) * BLOCK, :] = jnp.where(tile < 0, -1, col)

    @pl.when(ctx < 1)
    def _():
        kv_all[BLOCK:HALO, :] = jnp.zeros((HALO - BLOCK, kv_all.shape[1]), BF)

    @pl.when(ctx < 2)
    def _():
        kv_all[0:BLOCK, :] = jnp.zeros((BLOCK, kv_all.shape[1]), BF)

    @pl.when(ctx >= n_ctx - 1)
    def _():
        ghalo_in[BLOCK:HALO, :] = jnp.zeros((HALO - BLOCK, kv_all.shape[1]), BF)

    @pl.when(ctx >= n_ctx - 2)
    def _():
        ghalo_in[0:BLOCK, :] = jnp.zeros((BLOCK, kv_all.shape[1]), BF)

    gkv[...] = jnp.zeros_like(gkv)
    loads[0].wait()
    for c in range(model // BLOCK):
        flipped = tok[:, c * BLOCK : (c + 1) * BLOCK].T
        at = c * BLOCK
        while at < (c + 1) * BLOCK:
            shard = at // rows
            upto = min((shard + 1) * rows, (c + 1) * BLOCK)
            low = (shard // 2) * rows + at - shard * rows
            tok_all[0, shard % 2, low : low + upto - at, :] = flipped[at - c * BLOCK : upto - c * BLOCK]
            at = upto

    loads[1].wait()
    kv_all[HALO:, :] = dot(tok[...], wkv[...]).astype(BF)
    pl.semaphore_wait(barrier, n_dp + n_z)

    def tok_copy(origin, slot, k, half):
        return remote(tok_all.at[origin, half], tok_all.at[slot, half], tok_s.at[slot - 1, half],
                      tok_r.at[slot - 1, half], dp_peer(k), ctx)

    tok_copies = {}
    for i in range(2):
        for k in range(1, 3 if relayed else n_dp):
            half = (i + k + 1) % 2
            tok_copies[k, half] = tok_copy(0, k, k, half)
            tok_copies[k, half].start()

    halo_copies = []
    for g in range(KV_HEADS):
        for i, part in enumerate((g, KV_HEADS + g)):
            c = slice(part * HEAD_DIM, (part + 1) * HEAD_DIM)
            one = remote(kv_all.at[HALO:, c], kv_all.at[BLOCK:HALO, c], halo_s.at[g, i, 0],
                         halo_r.at[g, i, 0], dp, lax.rem(ctx + 1, n_ctx))
            two = remote(kv_all.at[HALO + BLOCK :, c], kv_all.at[0:BLOCK, c], halo_s.at[g, i, 1],
                         halo_r.at[g, i, 1], dp, lax.rem(ctx + 2, n_ctx))
            halo_copies.append((one, two))

            @pl.when(ctx + 2 < n_ctx)
            def _():
                two.start()

            @pl.when(ctx + 1 < n_ctx)
            def _():
                one.start()

    loads[2].wait()
    for p in range(HEADS // 2):
        both = dot(tok[...], wq[:, 2 * p * HEAD_DIM : 2 * (p + 1) * HEAD_DIM]).astype(BF)
        q[2 * p] = both[:, :HEAD_DIM]
        q[2 * p + 1] = both[:, HEAD_DIM:]
    loads[3].wait()

    key_row = lax.broadcasted_iota(jnp.int32, (WINDOW, BLOCK), 0)
    query_col = lax.broadcasted_iota(jnp.int32, (WINDOW, BLOCK), 1)

    def attend(g, b):
        row0 = pl.multiple_of(b * BLOCK, BLOCK)
        kcol = slice(g * HEAD_DIM, (g + 1) * HEAD_DIM)
        vcol = slice((KV_HEADS + g) * HEAD_DIM, (KV_HEADS + g + 1) * HEAD_DIM)
        window = pl.ds(row0, WINDOW)
        block = pl.ds(row0, BLOCK)
        keys = kv_all[window, kcol]
        vals = kv_all[window, vcol]
        keys_t = keys.T
        vals_t = vals.T
        first = pl.multiple_of(ctx * tok_rows + b * BLOCK, BLOCK)
        same = ids_col[window, :] == seg_ref[0:1, pl.ds(first, BLOCK)]
        bias = jnp.where((key_row <= query_col + HALO) & same, 0.0, -1e30)
        bias = jnp.concatenate([bias, bias], axis=1)
        grad_key = jnp.zeros((WINDOW, HEAD_DIM), F32)
        grad_val = jnp.zeros((WINDOW, HEAD_DIM), F32)
        for pair in range(GROUP // 2):
            h = g * GROUP + 2 * pair
            cols = [slice((h + i) * HEAD_DIM, (h + i + 1) * HEAD_DIM) for i in range(2)]
            query = jnp.concatenate([q[h, block, :], q[h + 1, block, :]], axis=0)
            grad = jnp.concatenate([do[block, c] for c in cols], axis=0)
            masked = jnp.where(bias < 0.0, -1e30, dot(keys, query, NT) * SCALE)
            top = jnp.max(masked, axis=0, keepdims=True)
            expo = jnp.exp(masked - top)
            probs = expo * (1.0 / jnp.sum(expo, axis=0, keepdims=True))
            probs_low = probs.astype(BF)
            out_t = dot(vals_t, probs_low).astype(BF).astype(F32)
            delta = jnp.sum(out_t * grad.astype(F32).T, axis=0, keepdims=True)
            grad_scores = (probs * (dot(vals, grad, NT) - delta) * SCALE).astype(BF)
            grad_query = dot(keys_t, grad_scores).T.astype(BF)
            out = out_t.T.astype(BF)
            for i, c in enumerate(cols):
                ctx_ref[block, c] = out[i * BLOCK : (i + 1) * BLOCK]
                comb[h + i, block, :] = grad_query[i * BLOCK : (i + 1) * BLOCK]
            grad_key = grad_key + dot(grad_scores, query)
            grad_val = grad_val + dot(probs_low, grad)
        gkv[window, kcol] += grad_key
        gkv[window, vcol] += grad_val

    copies = {}

    def send_slot(s):
        for k in range(1, n_dp):
            copy = remote(comb.at[s * n_dp + dp_peer(k)], comb_in.at[s, k - 1],
                          comb_s.at[s, k - 1], comb_r.at[s, k - 1], dp_peer(k), ctx)
            copy.start()
            copies["comb", s, k] = copy

    def ready(s):
        last = (s + 1) * n_dp
        return 0 if last <= GROUP else 1 if last <= HEADS else 2

    gh_copies = []
    for g in range(KV_HEADS):
        for one, two in halo_copies[2 * g : 2 * g + 2]:
            @pl.when(ctx >= 1)
            def _():
                one.wait_recv()

            @pl.when(ctx >= 2)
            def _():
                two.wait_recv()

        @pl.loop(0, tok_rows // BLOCK)
        def _(b):
            attend(g, b)

        for i, part in enumerate((g, KV_HEADS + g)):
            c = slice(part * HEAD_DIM, (part + 1) * HEAD_DIM)
            ghalo_out[:, c] = gkv[0:HALO, c].astype(BF)
            one = remote(ghalo_out.at[BLOCK:HALO, c], ghalo_in.at[BLOCK:HALO, c],
                         gh_s.at[g, i, 0], gh_r.at[g, i, 0], dp, lax.rem(ctx + n_ctx - 1, n_ctx))
            two = remote(ghalo_out.at[0:BLOCK, c], ghalo_in.at[0:BLOCK, c],
                         gh_s.at[g, i, 1], gh_r.at[g, i, 1], dp, lax.rem(ctx + n_ctx - 2, n_ctx))
            gh_copies.append((one, two))

            @pl.when(ctx >= 2)
            def _():
                two.start()

            @pl.when(ctx >= 1)
            def _():
                one.start()

        if g == 0 and relayed:
            tok_copies[1, 0].wait_recv()
            tok_copies[3, 0] = tok_copy(1, 3, 2, 0)
            tok_copies[3, 0].start()
            tok_copies[2, 1].wait_recv()
            tok_copies[3, 1] = tok_copy(2, 3, 1, 1)
            tok_copies[3, 1].start()

        for s in range(slots):
            if ready(s) == g:
                send_slot(s)

    def finish_keyval():
        for one, two in gh_copies:
            @pl.when(ctx + 1 < n_ctx)
            def _():
                one.wait_recv()

            @pl.when(ctx + 2 < n_ctx)
            def _():
                two.wait_recv()

        for part in range(2 * KV_HEADS):
            c = slice(part * HEAD_DIM, (part + 1) * HEAD_DIM)
            near = gkv[HALO:, c] + ghalo_in[BLOCK:HALO, c].astype(F32)
            comb[HEADS + part, 0:BLOCK, :] = near[0:BLOCK].astype(BF)
            comb[HEADS + part, BLOCK:, :] = (near[BLOCK:] + ghalo_in[0:BLOCK, c].astype(F32)).astype(BF)
        for s in range(slots):
            if ready(s) == 2:
                send_slot(s)

    def partial(s, parity):
        total = dot(tok_all[0, parity], comb[s * n_dp + dp])
        for k in range(1, n_dp):
            total = total + dot(tok_all[k, parity], comb_in[s, k - 1])
        return total

    def multiply(s):
        for k in range(1, n_dp):
            copies["comb", s, k].wait_recv()
        pair_out[s] = partial(s, 1 - core).astype(BF)
        copy = remote(pair_out.at[s], pair_in.at[s], pair_s.at[s], pair_r.at[s], dp, mate)
        copy.start()
        copies["pair", s] = copy
        part_own[s] = partial(s, core)

    def spread(s):
        copies["pair", s].wait_recv()
        z_out[s] = (part_own[s] + pair_in[s].astype(F32)).astype(BF)
        for k in range(1, n_z):
            piece = pl.ds(pl.multiple_of(z_peer(k) * rows, 16), rows)
            copy = remote(z_out.at[s, piece], z_in.at[s, k - 1], z_s.at[s, k - 1], z_r.at[s, k - 1],
                          dp, 2 * z_peer(k) + core)
            copy.start()
            copies["z", s, k] = copy

    def collect(s):
        mine = pl.ds(pl.multiple_of(level * rows, 16), rows)
        total = part_own[s, mine] + pair_in[s, mine].astype(F32)
        for k in range(1, n_z):
            copies["z", s, k].wait_recv()
            total = total + z_in[s, k - 1].astype(F32)
        spot = s * n_dp + dp
        gath[spot] = total.astype(BF)
        for k in range(1, n_dp):
            copy = remote(gath.at[spot], gath.at[spot], fin_s.at[s, k - 1], fin_r.at[s, k - 1],
                          dp_peer(k), ctx)
            copy.start()
            copies["fin", s, k] = copy

    def grad_in(low, high, last):
        @pl.loop(0, model // 256)
        def _(r):
            part = pl.ds(pl.multiple_of(r * 256, 256), 256)
            total = gi_acc[r] if last else jnp.zeros((256, tok_rows), F32)
            for p in range(low, high, 2):
                pairs = jnp.concatenate([comb[p], comb[p + 1]], axis=1)
                if p < HEADS:
                    weight = wq[part, p * HEAD_DIM : (p + 2) * HEAD_DIM]
                else:
                    weight = wkv[part, (p - HEADS) * HEAD_DIM : (p + 2 - HEADS) * HEAD_DIM]
                total = total + dot(weight, pairs, NT)
            if last:
                gi_ref[:, part] = total.T.astype(BF)
            else:
                gi_acc[r] = total

    early = [s for s in range(slots) if ready(s) < 2]
    late = [s for s in range(slots) if ready(s) == 2]
    order = early + late
    grad_in(0, HEADS, False)
    finish_keyval()
    grad_in(HEADS, COLUMNS, True)
    for (k, half), copy in tok_copies.items():
        if not relayed or (k, half) not in ((1, 0), (2, 1)):
            copy.wait_recv()
    for i in range(slots + 1):
        if i < slots:
            multiply(order[i])
        if i > 0:
            spread(order[i - 1])
    for s in order:
        collect(s)
    for name, copy in copies.items():
        if name[0] == "fin":
            copy.wait_recv()
    for j in range(COLUMNS):
        if j < HEADS:
            gwq_ref[:, j * HEAD_DIM : (j + 1) * HEAD_DIM] = gath[j]
        else:
            gwkv_ref[:, (j - HEADS) * HEAD_DIM : (j - HEADS + 1) * HEAD_DIM] = gath[j]
    for copy in list(copies.values()) + list(tok_copies.values()):
        copy.wait_send()
    for one, two in halo_copies:
        @pl.when(ctx + 1 < n_ctx)
        def _():
            one.wait_send()

        @pl.when(ctx + 2 < n_ctx)
        def _():
            two.wait_send()

    for one, two in gh_copies:
        @pl.when(ctx >= 1)
        def _():
            one.wait_send()

        @pl.when(ctx >= 2)
        def _():
            two.wait_send()


def square_kernel(
    n_ctx,
    tok_hbm, seg_ref, wq_hbm, wkv_hbm, do_hbm,
    ctx_ref, gi_ref, gwq_ref, gwkv_ref,
    tok, wq, wkv, do, tok_own, tok_in, q, kv_all, flip_all, ids_col, bias_ref, gkv, ghalo_out, ghalo_in,
    comb, comb_in, pair_out, pair_in, part_own, half_out, half_in, z_out, z_in, gath, gi_acc,
    load_s, tok_s, tok_r, halo_s, halo_r, gh_s, gh_r, comb_s, comb_r,
    pair_s, pair_r, half_s, half_r, z_s, z_r, fin_s, fin_r,
):
    n_z = n_ctx // 2
    n_h = n_z // 2
    tok_rows, model = tok.shape
    blocks = tok_rows // BLOCK
    dp = lax.axis_index("dp")
    ctx = lax.axis_index("ctx")
    core = lax.rem(ctx, 2)
    mate = ctx + 1 - 2 * core
    other = lax.rem(ctx + 2 * core - 1 + n_ctx, n_ctx)
    level = ctx // 2
    rows = gwq_ref.shape[0]
    part = rows // 2
    fast, slow = dp % 2, dp // 2
    place = ((fast, slow), (slow, fast))
    peers = (dp + 1 - 2 * fast, dp + 2 - 4 * slow, 3 - dp)
    top_half = level < n_h
    own_first = jnp.where(top_half, fast, slow)
    own_second = jnp.where(top_half, slow, fast)

    slots = [(0, 2), (4, 2), (8, 2), (HEADS, 1), (HEADS + 2, 1)]
    offsets = [0, 2, 4, 6, 7]

    def z_peer(k):
        return lax.rem(level + k, n_z)

    def remote(src, dst, send, recv, to_dp, to_ctx):
        return pltpu.make_async_remote_copy(
            src_ref=src, dst_ref=dst, send_sem=send, recv_sem=recv,
            device_id=(to_dp, to_ctx), device_id_type=MESH,
        )

    barrier = pltpu.get_barrier_semaphore()
    for peer in peers:
        pl.semaphore_signal(barrier, inc=1, device_id=(peer, ctx), device_id_type=MESH)
    for k in range(1, n_z):
        pl.semaphore_signal(
            barrier, inc=1, device_id=(dp, 2 * z_peer(k) + core), device_id_type=MESH
        )
    for to in (mate, other):
        pl.semaphore_signal(barrier, inc=1, device_id=(dp, to), device_id_type=MESH)

    loads = [
        pltpu.make_async_copy(src, dst, load_s.at[i])
        for i, (src, dst) in enumerate(
            [(tok_hbm, tok), (wkv_hbm, wkv), (wq_hbm, wq), (do_hbm, do)]
        )
    ]
    for copy in loads:
        copy.start()

    @pl.when(ctx < 1)
    def _():
        kv_all[BLOCK:HALO, :] = jnp.zeros((HALO - BLOCK, kv_all.shape[1]), BF)

    @pl.when(ctx < 2)
    def _():
        kv_all[0:BLOCK, :] = jnp.zeros((BLOCK, kv_all.shape[1]), BF)

    @pl.when(ctx >= n_ctx - 1)
    def _():
        ghalo_in[BLOCK:HALO, :] = jnp.zeros((HALO - BLOCK, kv_all.shape[1]), BF)

    @pl.when(ctx >= n_ctx - 2)
    def _():
        ghalo_in[0:BLOCK, :] = jnp.zeros((BLOCK, kv_all.shape[1]), BF)

    loads[0].wait()
    for c in range(model // BLOCK):
        flipped = tok[:, c * BLOCK : (c + 1) * BLOCK].T
        at = c * BLOCK
        while at < (c + 1) * BLOCK:
            shard = at // rows
            upto = min((shard + 1) * rows, (c + 1) * BLOCK)
            z = shard // 2
            low = (z % n_h) * rows + at - shard * rows
            tok_own[z // n_h, shard % 2, low : low + upto - at, :] = flipped[at - c * BLOCK : upto - c * BLOCK]
            at = upto
    loads[1].wait()
    kv_all[HALO:, :] = dot(tok[...], wkv[...]).astype(BF)
    pl.semaphore_wait(barrier, 4 + n_z)

    halo_copies = []
    for g in range(KV_HEADS):
        for i, piece in enumerate((g, KV_HEADS + g)):
            c = slice(piece * HEAD_DIM, (piece + 1) * HEAD_DIM)
            one = remote(kv_all.at[HALO:, c], kv_all.at[BLOCK:HALO, c], halo_s.at[g, i, 0],
                         halo_r.at[g, i, 0], dp, lax.rem(ctx + 1, n_ctx))
            two = remote(kv_all.at[HALO + BLOCK :, c], kv_all.at[0:BLOCK, c], halo_s.at[g, i, 1],
                         halo_r.at[g, i, 1], dp, lax.rem(ctx + 2, n_ctx))
            halo_copies.append((one, two))

    def start_halo(g):
        for one, _ in halo_copies[2 * g : 2 * g + 2]:
            @pl.when(ctx + 1 < n_ctx)
            def _():
                one.start()

        for _, two in halo_copies[2 * g : 2 * g + 2]:
            @pl.when(ctx + 2 < n_ctx)
            def _():
                two.start()

    tok_copies = [
        remote(tok_own.at[r], tok_in.at[r], tok_s.at[r], tok_r.at[r], peers[r], ctx) for r in range(2)
    ]
    start_halo(0)
    for copy in tok_copies:
        copy.start()
    start_halo(1)

    tile0 = ctx * blocks - HALO // BLOCK
    for t in range(HALO // BLOCK + blocks):
        tile = tile0 + t
        start = pl.multiple_of(jnp.maximum(tile, 0) * BLOCK, BLOCK)
        row = seg_ref[0:1, pl.ds(start, BLOCK)]
        col = jnp.broadcast_to(row, (BLOCK, BLOCK)).T
        ids_col[t * BLOCK : (t + 1) * BLOCK, :] = jnp.where(tile < 0, -1, col)
    key_row = lax.broadcasted_iota(jnp.int32, (WINDOW, BLOCK), 0)
    query_col = lax.broadcasted_iota(jnp.int32, (WINDOW, BLOCK), 1)
    for b in range(blocks):
        first = pl.multiple_of(ctx * tok_rows + b * BLOCK, BLOCK)
        same = ids_col[b * BLOCK : b * BLOCK + WINDOW, :] == seg_ref[0:1, pl.ds(first, BLOCK)]
        bias_ref[b] = jnp.where((key_row <= query_col + HALO) & same, 0.0, -1e30)

    gkv[...] = jnp.zeros_like(gkv)
    loads[2].wait()
    for p in range(HEADS // 2):
        both = dot(tok[...], wq[:, 2 * p * HEAD_DIM : 2 * (p + 1) * HEAD_DIM]).astype(BF)
        q[2 * p] = both[:, :HEAD_DIM]
        q[2 * p + 1] = both[:, HEAD_DIM:]
    loads[3].wait()

    def columns(g):
        return [slice(j * HEAD_DIM, (j + 1) * HEAD_DIM) for j in (g, KV_HEADS + g)]

    def attend(g, p, b):
        row0 = b * BLOCK
        kcol, vcol = columns(g)
        window = slice(row0, row0 + WINDOW)
        block = slice(row0, row0 + BLOCK)
        keys = kv_all[window, kcol]
        vals = kv_all[window, vcol]
        keys_t = flip_all[0, :, window]
        vals_t = flip_all[1, :, window]
        bias = bias_ref[b]
        bias = jnp.concatenate([bias, bias], axis=1)
        h = g * GROUP + 2 * p
        cols = [slice((h + i) * HEAD_DIM, (h + i + 1) * HEAD_DIM) for i in range(2)]
        query = jnp.concatenate([q[h, block, :], q[h + 1, block, :]], axis=0)
        grad = jnp.concatenate([do[block, c] for c in cols], axis=0)
        masked = dot(keys, query, NT) * SCALE + bias
        top = jnp.max(masked, axis=0, keepdims=True)
        expo = jnp.exp(masked - top)
        probs = expo * (1.0 / jnp.sum(expo, axis=0, keepdims=True))
        probs_low = probs.astype(BF)
        out_t = dot(vals_t, probs_low).astype(BF).astype(F32)
        delta = jnp.sum(out_t * grad.astype(F32).T, axis=0, keepdims=True)
        grad_scores = (probs * (dot(vals, grad, NT) - delta) * SCALE).astype(BF)
        grad_query = dot(keys_t, grad_scores).T.astype(BF)
        out = out_t.T.astype(BF)
        for i, c in enumerate(cols):
            ctx_ref[block, c] = out[i * BLOCK : (i + 1) * BLOCK]
            comb[h + i, block, :] = grad_query[i * BLOCK : (i + 1) * BLOCK]
        gkv[window, kcol] += dot(grad_scores, query)
        gkv[window, vcol] += dot(probs_low, grad)

    copies = {}

    def near_halo(g):
        for i, c in enumerate(columns(g)):
            flip_all[i, :, HALO:] = kv_all[HALO:, c].T
        for one, _ in halo_copies[2 * g : 2 * g + 2]:
            @pl.when(ctx >= 1)
            def _():
                one.wait_recv()

        for i, c in enumerate(columns(g)):
            flip_all[i, :, BLOCK:HALO] = kv_all[BLOCK:HALO, c].T

    def far_halo(g):
        for _, two in halo_copies[2 * g : 2 * g + 2]:
            @pl.when(ctx >= 2)
            def _():
                two.wait_recv()

        for i, c in enumerate(columns(g)):
            flip_all[i, :, 0:BLOCK] = kv_all[0:BLOCK, c].T

    gh_copies = {}

    def send_halo(g):
        gh_copies[g] = []
        for i, c in enumerate(columns(g)):
            ghalo_out[:, c] = gkv[0:HALO, c].astype(BF)
            one = remote(ghalo_out.at[BLOCK:HALO, c], ghalo_in.at[BLOCK:HALO, c],
                         gh_s.at[g, i, 0], gh_r.at[g, i, 0], dp, lax.rem(ctx + n_ctx - 1, n_ctx))
            two = remote(ghalo_out.at[0:BLOCK, c], ghalo_in.at[0:BLOCK, c],
                         gh_s.at[g, i, 1], gh_r.at[g, i, 1], dp, lax.rem(ctx + n_ctx - 2, n_ctx))
            gh_copies[g].append((one, two))

            @pl.when(ctx >= 2)
            def _():
                two.start()

            @pl.when(ctx >= 1)
            def _():
                one.start()

    def finish_keyval(g):
        for one, two in gh_copies[g]:
            @pl.when(ctx + 1 < n_ctx)
            def _():
                one.wait_recv()

            @pl.when(ctx + 2 < n_ctx)
            def _():
                two.wait_recv()

        for i, c in enumerate(columns(g)):
            near = gkv[HALO:, c] + ghalo_in[BLOCK:HALO, c].astype(F32)
            at = HEADS + 2 * g + i
            comb[at, 0:BLOCK, :] = near[0:BLOCK].astype(BF)
            comb[at, BLOCK:, :] = (near[BLOCK:] + ghalo_in[0:BLOCK, c].astype(F32)).astype(BF)

    def send_slot(s):
        (low, width), at = slots[s], offsets[s]
        for r in range(2):
            theirs = pl.ds(low + width * (1 - place[r][0]), width)
            copy = remote(comb.at[theirs], comb_in.at[r, at : at + width], comb_s.at[s, r], comb_r.at[s, r],
                          peers[r], ctx)
            copy.start()
            copies["comb", s, r] = copy

    def multiply(s):
        (low, width), at = slots[s], offsets[s]
        for r in range(2):
            copies["comb", s, r].wait_recv()

        def product(r, parity):
            mine = [comb[low + width * place[r][0] + i] for i in range(width)]
            theirs = [comb_in[r, at + i] for i in range(width)]
            total = dot(tok_own[r, parity], jnp.concatenate(mine, axis=1))
            total = total + dot(tok_in[r, parity], jnp.concatenate(theirs, axis=1))
            return [total[:, i * HEAD_DIM : (i + 1) * HEAD_DIM] for i in range(width)]

        for r in range(2):
            for i, piece in enumerate(product(r, 1 - core)):
                pair_out[at + i, r] = piece.astype(BF)
        copy = remote(pair_out.at[at : at + width], pair_in.at[at : at + width], pair_s.at[s], pair_r.at[s],
                      dp, mate)
        copy.start()
        copies["pair", s] = copy
        for r in range(2):
            for i, piece in enumerate(product(r, core)):
                part_own[at + i, r] = piece

    def halve(s):
        (_, width), at = slots[s], offsets[s]
        copies["pair", s].wait_recv()
        for r in range(2):
            for i in range(at, at + width):
                for z in range(n_h):
                    away = pl.ds(pl.multiple_of(z * rows + (1 - place[r][1]) * part, 16), part)
                    total = part_own[i, r, away] + pair_in[i, r, away].astype(F32)
                    half_out[r, i, z] = total.astype(BF)
            copy = remote(half_out.at[r, at : at + width], half_in.at[r, at : at + width], half_s.at[s, r],
                          half_r.at[s, r], peers[1 - r], ctx)
            copy.start()
            copies["half", s, r] = copy

    def spread(s):
        (_, width), at = slots[s], offsets[s]
        for r in range(2):
            copies["half", s, r].wait_recv()
        for r in range(2):
            for z in range(n_h):
                for i in range(at, at + width):
                    here = pl.ds(pl.multiple_of(z * rows + place[r][1] * part, 16), part)
                    total = part_own[i, r, here] + pair_in[i, r, here].astype(F32)
                    total = total + half_in[r, i, z].astype(F32)
                    z_out[r * n_h + z, i] = total.astype(BF)
        for k in range(1, n_z):
            copy = remote(z_out.at[z_peer(k), at : at + width], z_in.at[k - 1, at : at + width],
                          z_s.at[s, k - 1], z_r.at[s, k - 1], dp, 2 * z_peer(k) + core)
            copy.start()
            copies["z", s, k] = copy

    def collect(s):
        (low, width), at = slots[s], offsets[s]
        r, z = level // n_h, lax.rem(level, n_h)
        here = pl.ds(pl.multiple_of(z * rows + own_second * part, 16), part)
        totals = [
            part_own[i, r, here] + pair_in[i, r, here].astype(F32) + half_in[r, i, z].astype(F32)
            for i in range(at, at + width)
        ]
        for k in range(1, n_z):
            copies["z", s, k].wait_recv()
            totals = [total + z_in[k - 1, at + i].astype(F32) for i, total in enumerate(totals)]
        spot = pl.ds(pl.multiple_of(own_second * part, 16), part)
        for i, total in enumerate(totals):
            gath[low + width * own_first + i, spot, :] = total.astype(BF)
        held = gath.at[pl.ds(low + width * own_first, width), spot, :]
        for k, peer in enumerate(peers):
            copy = remote(held, held, fin_s.at[s, k], fin_r.at[s, k], peer, ctx)
            copy.start()
            copies["fin", s, k] = copy

    def grad_in(r, low, high, last):
        rows_in = slice(r * 256, (r + 1) * 256)
        total = gi_acc[r] if low else jnp.zeros((256, tok_rows), F32)
        for p in range(low, high, 2):
            pairs = jnp.concatenate([comb[p], comb[p + 1]], axis=1)
            if p < HEADS:
                weight = wq[rows_in, p * HEAD_DIM : (p + 2) * HEAD_DIM]
            else:
                weight = jnp.concatenate([wkv[rows_in, c] for c in columns((p - HEADS) // 2)], axis=1)
            total = total + dot(weight, pairs, NT)
        if last:
            gi_ref[:, rows_in] = total.T.astype(BF)
        else:
            gi_acc[r] = total

    def attend_pair(g, p):
        for b in reversed(range(blocks)):
            if p == 0 and b == 0:
                far_halo(g)
            attend(g, p, b)

    def tokens_in():
        for copy in tok_copies:
            copy.wait_recv()

    def grad_in_heads(r):
        grad_in(r, 0, HEADS, False)

    def grad_in_rest():
        for r in range(model // 256):
            grad_in(r, HEADS, COLUMNS, True)

    schedule = (
        (near_halo, 0), (attend_pair, 0, 0), (attend_pair, 0, 1), (send_slot, 0), (attend_pair, 0, 2),
        (send_halo, 0), (near_halo, 1), (attend_pair, 1, 0), (send_slot, 1), (attend_pair, 1, 1),
        (tokens_in,), (multiply, 0), (finish_keyval, 0), (send_slot, 3), (attend_pair, 1, 2),
        (send_halo, 1), (send_slot, 2), (halve, 0), (multiply, 1), (grad_in_heads, 0), (halve, 1),
        (grad_in_heads, 1), (multiply, 3), (grad_in_heads, 2), (finish_keyval, 1), (send_slot, 4), (halve, 3),
        (spread, 0), (multiply, 2), (grad_in_heads, 3), (halve, 2), (spread, 1), (multiply, 4), (collect, 0),
        (halve, 4), (spread, 3), (grad_in_heads, 4), (spread, 2), (collect, 1), (grad_in_heads, 5),
        (spread, 4), (collect, 3), (grad_in_rest,), (collect, 2), (collect, 4),
    )
    for step, *operands in schedule:
        step(*operands)
    for name, copy in copies.items():
        if name[0] == "fin":
            copy.wait_recv()
    for j in range(COLUMNS):
        if j < HEADS:
            gwq_ref[:, j * HEAD_DIM : (j + 1) * HEAD_DIM] = gath[j]
        else:
            at = KV_HEADS * ((j - HEADS) % 2) + (j - HEADS) // 2
            gwkv_ref[:, at * HEAD_DIM : (at + 1) * HEAD_DIM] = gath[j]
    for copy in list(copies.values()) + tok_copies:
        copy.wait_send()
    for one, two in halo_copies:
        @pl.when(ctx + 1 < n_ctx)
        def _():
            one.wait_send()

        @pl.when(ctx + 2 < n_ctx)
        def _():
            two.wait_send()

    for g in range(KV_HEADS):
        for one, two in gh_copies[g]:
            @pl.when(ctx >= 1)
            def _():
                one.wait_send()

            @pl.when(ctx >= 2)
            def _():
                two.wait_send()


def copy_kernel(*refs):
    count = (len(refs) - 1) // 2
    sources, targets, sems = refs[:count], refs[count : 2 * count], refs[-1]
    leave = [pltpu.make_async_copy(sources[i], targets[i], sems.at[i]) for i in range(count)]
    for copy in leave:
        copy.start()
    for copy in leave:
        copy.wait()


def copied(arrays):
    hbm = pl.BlockSpec(memory_space=pltpu.MemorySpace.HBM)
    return pl.pallas_call(
        copy_kernel,
        out_shape=tuple(jax.ShapeDtypeStruct(a.shape, a.dtype) for a in arrays),
        in_specs=[pl.BlockSpec(memory_space=pl.ANY)] * len(arrays),
        out_specs=(hbm,) * len(arrays),
        scratch_shapes=[pltpu.SemaphoreType.DMA((len(arrays),))],
        compiler_params=pltpu.CompilerParams(vmem_limit_bytes=1024 * 1024),
        name="results",
    )(*arrays)


def square_scratch(n_ctx, tok_rows, model, kv_cols):
    n_z = n_ctx // 2
    n_h = n_z // 2
    rows = model // n_ctx
    part = rows // 2
    keys = HALO + tok_rows
    held = COLUMNS // 2
    dma = pltpu.SemaphoreType.DMA
    return [
        pltpu.VMEM((tok_rows, model), BF),
        pltpu.VMEM((model, model), BF),
        pltpu.VMEM((model, kv_cols), BF),
        pltpu.VMEM((tok_rows, model), BF),
        pltpu.VMEM((2, 2, n_h * rows, tok_rows), BF),
        pltpu.VMEM((2, 2, n_h * rows, tok_rows), BF),
        pltpu.VMEM((HEADS, tok_rows, HEAD_DIM), BF),
        pltpu.VMEM((keys, kv_cols), BF),
        pltpu.VMEM((2, HEAD_DIM, keys), BF),
        pltpu.VMEM((keys, BLOCK), jnp.int32),
        pltpu.VMEM((tok_rows // BLOCK, WINDOW, BLOCK), F32),
        pltpu.VMEM((keys, kv_cols), F32),
        pltpu.VMEM((HALO, kv_cols), BF),
        pltpu.VMEM((HALO, kv_cols), BF),
        pltpu.VMEM((COLUMNS, tok_rows, HEAD_DIM), BF),
        pltpu.VMEM((2, held, tok_rows, HEAD_DIM), BF),
        pltpu.VMEM((held, 2, n_h * rows, HEAD_DIM), BF),
        pltpu.VMEM((held, 2, n_h * rows, HEAD_DIM), BF),
        pltpu.VMEM((held, 2, n_h * rows, HEAD_DIM), F32),
        pltpu.VMEM((2, held, n_h, part, HEAD_DIM), BF),
        pltpu.VMEM((2, held, n_h, part, HEAD_DIM), BF),
        pltpu.VMEM((n_z, held, part, HEAD_DIM), BF),
        pltpu.VMEM((n_z - 1, held, part, HEAD_DIM), BF),
        pltpu.VMEM((COLUMNS, rows, HEAD_DIM), BF),
        pltpu.VMEM((model // 256, 256, tok_rows), F32),
        dma((4,)),
        dma((2,)), dma((2,)),
        dma((KV_HEADS, 2, 2)), dma((KV_HEADS, 2, 2)),
        dma((KV_HEADS, 2, 2)), dma((KV_HEADS, 2, 2)),
        dma((5, 2)), dma((5, 2)),
        dma((5,)), dma((5,)),
        dma((5, 2)), dma((5, 2)),
        dma((5, n_z - 1)), dma((5, n_z - 1)),
        dma((5, 3)), dma((5, 3)),
    ]


def shards(tokens, segments, w_query, w_keyval, grad_context):
    hidden_in = tokens[0]
    tok_rows, model = hidden_in.shape
    kv_cols = w_keyval.shape[1]
    n_ctx = lax.axis_size("ctx")
    n_dp = lax.axis_size("dp")
    n_z = n_ctx // 2
    rows = model // n_ctx
    slots = COLUMNS // n_dp
    half = n_z * rows
    square = n_dp == 4 and n_ctx % 4 == 0 and rows % 32 == 0
    keys = HALO + tok_rows
    vmem = pl.BlockSpec(memory_space=pltpu.VMEM)
    hbm = pl.BlockSpec(memory_space=pltpu.MemorySpace.HBM)
    dma = pltpu.SemaphoreType.DMA
    results = pl.pallas_call(
        functools.partial(square_kernel, n_ctx) if square else functools.partial(layer_kernel, n_dp, n_ctx),
        out_shape=(
            pltpu.VMEM((tok_rows, model), BF),
            pltpu.VMEM((tok_rows, model), BF),
            pltpu.VMEM((rows, model), BF),
            pltpu.VMEM((rows, kv_cols), BF),
        ),
        in_specs=[hbm, vmem, hbm, hbm, hbm],
        out_specs=(vmem,) * 4,
        scratch_shapes=square_scratch(n_ctx, tok_rows, model, kv_cols) if square else [
            pltpu.VMEM((tok_rows, model), BF),
            pltpu.VMEM((model, model), BF),
            pltpu.VMEM((model, kv_cols), BF),
            pltpu.VMEM((tok_rows, model), BF),
            pltpu.VMEM((n_dp, 2, half, tok_rows), BF),
            pltpu.VMEM((HEADS, tok_rows, HEAD_DIM), BF),
            pltpu.VMEM((keys, kv_cols), BF),
            pltpu.VMEM((keys, BLOCK), jnp.int32),
            pltpu.VMEM((keys, kv_cols), F32),
            pltpu.VMEM((HALO, kv_cols), BF),
            pltpu.VMEM((HALO, kv_cols), BF),
            pltpu.VMEM((COLUMNS, tok_rows, HEAD_DIM), BF),
            pltpu.VMEM((slots, n_dp - 1, tok_rows, HEAD_DIM), BF),
            pltpu.VMEM((slots, half, HEAD_DIM), BF),
            pltpu.VMEM((slots, half, HEAD_DIM), BF),
            pltpu.VMEM((slots, half, HEAD_DIM), F32),
            pltpu.VMEM((slots, half, HEAD_DIM), BF),
            pltpu.VMEM((slots, n_z - 1, rows, HEAD_DIM), BF),
            pltpu.VMEM((COLUMNS, rows, HEAD_DIM), BF),
            pltpu.VMEM((model // 256, 256, tok_rows), F32),
            dma((4,)),
            dma((n_dp - 1, 2)), dma((n_dp - 1, 2)),
            dma((KV_HEADS, 2, 2)), dma((KV_HEADS, 2, 2)),
            dma((KV_HEADS, 2, 2)), dma((KV_HEADS, 2, 2)),
            dma((slots, n_dp - 1)), dma((slots, n_dp - 1)),
            dma((slots,)), dma((slots,)),
            dma((slots, n_z - 1)), dma((slots, n_z - 1)),
            dma((slots, n_dp - 1)), dma((slots, n_dp - 1)),
        ],
        compiler_params=pltpu.CompilerParams(
            collective_id=0, has_side_effects=True, vmem_limit_bytes=61 * 1024 * 1024
        ),
        name="layer",
    )(hidden_in, segments, w_query, w_keyval, grad_context[0])
    context, grad_in, grad_wq, grad_wkv = copied(results)
    return context[None], grad_in[None], grad_wq, grad_wkv


def solution(mesh):
    placed = (P("dp", "ctx", None), P("dp", None), P(), P(), P("dp", "ctx", None))
    return jax.shard_map(
        shards,
        mesh=mesh,
        in_specs=placed,
        out_specs=(P("dp", "ctx", None), P("dp", "ctx", None), P("ctx", None), P("ctx", None)),
        check_vma=False,
    )
```

```python
import functools

import jax
import jax.numpy as jnp
from jax import lax
from jax.experimental import pallas as pl
from jax.experimental.pallas import tpu as pltpu
from jax.sharding import PartitionSpec as P

HEADS = 12
KV_HEADS = 2
HEAD_DIM = 128
WINDOW = 512
BLOCK = 128
HALO = WINDOW - BLOCK
GROUP = HEADS // KV_HEADS
COLUMNS = HEADS + 2 * KV_HEADS
SCALE = HEAD_DIM ** (-0.5)
MESH = pl.DeviceIdType.MESH
NT = (((1,), (1,)), ((), ()))
NN = (((1,), (0,)), ((), ()))
BF = jnp.bfloat16
F32 = jnp.float32


def dot(a, b, dims=NN):
    return lax.dot_general(a, b, dims, preferred_element_type=F32)


def layer_kernel(
    n_dp, n_ctx,
    tok_hbm, seg_ref, wq_hbm, wkv_hbm, do_hbm,
    ctx_ref, gi_ref, gwq_ref, gwkv_ref,
    tok, wq, wkv, do, tok_all, q, kv_all, ids_col, gkv, ghalo_out, ghalo_in, comb, comb_in,
    pair_out, pair_in, part_own, z_out, z_in, gath, gi_acc,
    load_s, tok_s, tok_r, halo_s, halo_r, gh_s, gh_r, comb_s, comb_r,
    pair_s, pair_r, z_s, z_r, fin_s, fin_r,
):
    n_z = n_ctx // 2
    slots = COLUMNS // n_dp
    tok_rows, model = tok.shape
    dp = lax.axis_index("dp")
    ctx = lax.axis_index("ctx")
    core = lax.rem(ctx, 2)
    mate = ctx + 1 - 2 * core
    other = lax.rem(ctx + 2 * core - 1 + n_ctx, n_ctx)
    level = ctx // 2
    rows = gwq_ref.shape[0]

    relayed = n_dp == 4

    def dp_peer(k):
        if relayed:
            return (dp + 1 - 2 * (dp % 2), dp + 2 - 4 * (dp // 2), 3 - dp)[k - 1]
        return lax.rem(dp + k, n_dp)

    def z_peer(k):
        return lax.rem(level + k, n_z)

    def remote(src, dst, send, recv, to_dp, to_ctx):
        return pltpu.make_async_remote_copy(
            src_ref=src, dst_ref=dst, send_sem=send, recv_sem=recv,
            device_id=(to_dp, to_ctx), device_id_type=MESH,
        )

    barrier = pltpu.get_barrier_semaphore()
    for k in range(1, n_dp):
        pl.semaphore_signal(barrier, inc=1, device_id=(dp_peer(k), ctx), device_id_type=MESH)
    for k in range(1, n_z):
        pl.semaphore_signal(
            barrier, inc=1, device_id=(dp, 2 * z_peer(k) + core), device_id_type=MESH
        )
    for to in (mate, other):
        pl.semaphore_signal(barrier, inc=1, device_id=(dp, to), device_id_type=MESH)

    loads = [
        pltpu.make_async_copy(src, dst, load_s.at[i])
        for i, (src, dst) in enumerate(
            [(tok_hbm, tok), (wkv_hbm, wkv), (wq_hbm, wq), (do_hbm, do)]
        )
    ]
    for copy in loads:
        copy.start()

    tile0 = ctx * (tok_rows // BLOCK) - HALO // BLOCK
    for t in range((HALO + tok_rows) // BLOCK):
        tile = tile0 + t
        start = pl.multiple_of(jnp.maximum(tile, 0) * BLOCK, BLOCK)
        row = seg_ref[0:1, pl.ds(start, BLOCK)]
        col = jnp.broadcast_to(row, (BLOCK, BLOCK)).T
        ids_col[t * BLOCK : (t + 1) * BLOCK, :] = jnp.where(tile < 0, -1, col)

    @pl.when(ctx < 1)
    def _():
        kv_all[BLOCK:HALO, :] = jnp.zeros((HALO - BLOCK, kv_all.shape[1]), BF)

    @pl.when(ctx < 2)
    def _():
        kv_all[0:BLOCK, :] = jnp.zeros((BLOCK, kv_all.shape[1]), BF)

    @pl.when(ctx >= n_ctx - 1)
    def _():
        ghalo_in[BLOCK:HALO, :] = jnp.zeros((HALO - BLOCK, kv_all.shape[1]), BF)

    @pl.when(ctx >= n_ctx - 2)
    def _():
        ghalo_in[0:BLOCK, :] = jnp.zeros((BLOCK, kv_all.shape[1]), BF)

    gkv[...] = jnp.zeros_like(gkv)
    loads[0].wait()
    for c in range(model // BLOCK):
        flipped = tok[:, c * BLOCK : (c + 1) * BLOCK].T
        at = c * BLOCK
        while at < (c + 1) * BLOCK:
            shard = at // rows
            upto = min((shard + 1) * rows, (c + 1) * BLOCK)
            low = (shard // 2) * rows + at - shard * rows
            tok_all[0, shard % 2, low : low + upto - at, :] = flipped[at - c * BLOCK : upto - c * BLOCK]
            at = upto

    loads[1].wait()
    kv_all[HALO:, :] = dot(tok[...], wkv[...]).astype(BF)
    pl.semaphore_wait(barrier, n_dp + n_z)

    def tok_copy(origin, slot, k, half):
        return remote(tok_all.at[origin, half], tok_all.at[slot, half], tok_s.at[slot - 1, half],
                      tok_r.at[slot - 1, half], dp_peer(k), ctx)

    tok_copies = {}
    for i in range(2):
        for k in range(1, 3 if relayed else n_dp):
            half = (i + k + 1) % 2
            tok_copies[k, half] = tok_copy(0, k, k, half)
            tok_copies[k, half].start()

    halo_copies = []
    for g in range(KV_HEADS):
        for i, part in enumerate((g, KV_HEADS + g)):
            c = slice(part * HEAD_DIM, (part + 1) * HEAD_DIM)
            one = remote(kv_all.at[HALO:, c], kv_all.at[BLOCK:HALO, c], halo_s.at[g, i, 0],
                         halo_r.at[g, i, 0], dp, lax.rem(ctx + 1, n_ctx))
            two = remote(kv_all.at[HALO + BLOCK :, c], kv_all.at[0:BLOCK, c], halo_s.at[g, i, 1],
                         halo_r.at[g, i, 1], dp, lax.rem(ctx + 2, n_ctx))
            halo_copies.append((one, two))

            @pl.when(ctx + 2 < n_ctx)
            def _():
                two.start()

            @pl.when(ctx + 1 < n_ctx)
            def _():
                one.start()

    loads[2].wait()
    for p in range(HEADS // 2):
        both = dot(tok[...], wq[:, 2 * p * HEAD_DIM : 2 * (p + 1) * HEAD_DIM]).astype(BF)
        q[2 * p] = both[:, :HEAD_DIM]
        q[2 * p + 1] = both[:, HEAD_DIM:]
    loads[3].wait()

    key_row = lax.broadcasted_iota(jnp.int32, (WINDOW, BLOCK), 0)
    query_col = lax.broadcasted_iota(jnp.int32, (WINDOW, BLOCK), 1)

    def attend(g, b):
        row0 = pl.multiple_of(b * BLOCK, BLOCK)
        kcol = slice(g * HEAD_DIM, (g + 1) * HEAD_DIM)
        vcol = slice((KV_HEADS + g) * HEAD_DIM, (KV_HEADS + g + 1) * HEAD_DIM)
        window = pl.ds(row0, WINDOW)
        block = pl.ds(row0, BLOCK)
        keys = kv_all[window, kcol]
        vals = kv_all[window, vcol]
        keys_t = keys.T
        vals_t = vals.T
        first = pl.multiple_of(ctx * tok_rows + b * BLOCK, BLOCK)
        same = ids_col[window, :] == seg_ref[0:1, pl.ds(first, BLOCK)]
        bias = jnp.where((key_row <= query_col + HALO) & same, 0.0, -1e30)
        bias = jnp.concatenate([bias, bias], axis=1)
        grad_key = jnp.zeros((WINDOW, HEAD_DIM), F32)
        grad_val = jnp.zeros((WINDOW, HEAD_DIM), F32)
        for pair in range(GROUP // 2):
            h = g * GROUP + 2 * pair
            cols = [slice((h + i) * HEAD_DIM, (h + i + 1) * HEAD_DIM) for i in range(2)]
            query = jnp.concatenate([q[h, block, :], q[h + 1, block, :]], axis=0)
            grad = jnp.concatenate([do[block, c] for c in cols], axis=0)
            masked = jnp.where(bias < 0.0, -1e30, dot(keys, query, NT) * SCALE)
            top = jnp.max(masked, axis=0, keepdims=True)
            expo = jnp.exp(masked - top)
            probs = expo * (1.0 / jnp.sum(expo, axis=0, keepdims=True))
            probs_low = probs.astype(BF)
            out_t = dot(vals_t, probs_low).astype(BF).astype(F32)
            delta = jnp.sum(out_t * grad.astype(F32).T, axis=0, keepdims=True)
            grad_scores = (probs * (dot(vals, grad, NT) - delta) * SCALE).astype(BF)
            grad_query = dot(keys_t, grad_scores).T.astype(BF)
            out = out_t.T.astype(BF)
            for i, c in enumerate(cols):
                ctx_ref[block, c] = out[i * BLOCK : (i + 1) * BLOCK]
                comb[h + i, block, :] = grad_query[i * BLOCK : (i + 1) * BLOCK]
            grad_key = grad_key + dot(grad_scores, query)
            grad_val = grad_val + dot(probs_low, grad)
        gkv[window, kcol] += grad_key
        gkv[window, vcol] += grad_val

    copies = {}

    def send_slot(s):
        for k in range(1, n_dp):
            copy = remote(comb.at[s * n_dp + dp_peer(k)], comb_in.at[s, k - 1],
                          comb_s.at[s, k - 1], comb_r.at[s, k - 1], dp_peer(k), ctx)
            copy.start()
            copies["comb", s, k] = copy

    def ready(s):
        last = (s + 1) * n_dp
        return 0 if last <= GROUP else 1 if last <= HEADS else 2

    gh_copies = []
    for g in range(KV_HEADS):
        for one, two in halo_copies[2 * g : 2 * g + 2]:
            @pl.when(ctx >= 1)
            def _():
                one.wait_recv()

            @pl.when(ctx >= 2)
            def _():
                two.wait_recv()

        @pl.loop(0, tok_rows // BLOCK)
        def _(b):
            attend(g, b)

        for i, part in enumerate((g, KV_HEADS + g)):
            c = slice(part * HEAD_DIM, (part + 1) * HEAD_DIM)
            ghalo_out[:, c] = gkv[0:HALO, c].astype(BF)
            one = remote(ghalo_out.at[BLOCK:HALO, c], ghalo_in.at[BLOCK:HALO, c],
                         gh_s.at[g, i, 0], gh_r.at[g, i, 0], dp, lax.rem(ctx + n_ctx - 1, n_ctx))
            two = remote(ghalo_out.at[0:BLOCK, c], ghalo_in.at[0:BLOCK, c],
                         gh_s.at[g, i, 1], gh_r.at[g, i, 1], dp, lax.rem(ctx + n_ctx - 2, n_ctx))
            gh_copies.append((one, two))

            @pl.when(ctx >= 2)
            def _():
                two.start()

            @pl.when(ctx >= 1)
            def _():
                one.start()

        if g == 0 and relayed:
            tok_copies[1, 0].wait_recv()
            tok_copies[3, 0] = tok_copy(1, 3, 2, 0)
            tok_copies[3, 0].start()
            tok_copies[2, 1].wait_recv()
            tok_copies[3, 1] = tok_copy(2, 3, 1, 1)
            tok_copies[3, 1].start()

        for s in range(slots):
            if ready(s) == g:
                send_slot(s)

    def finish_keyval():
        for one, two in gh_copies:
            @pl.when(ctx + 1 < n_ctx)
            def _():
                one.wait_recv()

            @pl.when(ctx + 2 < n_ctx)
            def _():
                two.wait_recv()

        for part in range(2 * KV_HEADS):
            c = slice(part * HEAD_DIM, (part + 1) * HEAD_DIM)
            near = gkv[HALO:, c] + ghalo_in[BLOCK:HALO, c].astype(F32)
            comb[HEADS + part, 0:BLOCK, :] = near[0:BLOCK].astype(BF)
            comb[HEADS + part, BLOCK:, :] = (near[BLOCK:] + ghalo_in[0:BLOCK, c].astype(F32)).astype(BF)
        for s in range(slots):
            if ready(s) == 2:
                send_slot(s)

    def partial(s, parity):
        total = dot(tok_all[0, parity], comb[s * n_dp + dp])
        for k in range(1, n_dp):
            total = total + dot(tok_all[k, parity], comb_in[s, k - 1])
        return total

    def multiply(s):
        for k in range(1, n_dp):
            copies["comb", s, k].wait_recv()
        pair_out[s] = partial(s, 1 - core).astype(BF)
        copy = remote(pair_out.at[s], pair_in.at[s], pair_s.at[s], pair_r.at[s], dp, mate)
        copy.start()
        copies["pair", s] = copy
        part_own[s] = partial(s, core)

    def spread(s):
        copies["pair", s].wait_recv()
        z_out[s] = (part_own[s] + pair_in[s].astype(F32)).astype(BF)
        for k in range(1, n_z):
            piece = pl.ds(pl.multiple_of(z_peer(k) * rows, 16), rows)
            copy = remote(z_out.at[s, piece], z_in.at[s, k - 1], z_s.at[s, k - 1], z_r.at[s, k - 1],
                          dp, 2 * z_peer(k) + core)
            copy.start()
            copies["z", s, k] = copy

    def collect(s):
        mine = pl.ds(pl.multiple_of(level * rows, 16), rows)
        total = part_own[s, mine] + pair_in[s, mine].astype(F32)
        for k in range(1, n_z):
            copies["z", s, k].wait_recv()
            total = total + z_in[s, k - 1].astype(F32)
        spot = s * n_dp + dp
        gath[spot] = total.astype(BF)
        for k in range(1, n_dp):
            copy = remote(gath.at[spot], gath.at[spot], fin_s.at[s, k - 1], fin_r.at[s, k - 1],
                          dp_peer(k), ctx)
            copy.start()
            copies["fin", s, k] = copy

    def grad_in(low, high, last):
        @pl.loop(0, model // 256)
        def _(r):
            part = pl.ds(pl.multiple_of(r * 256, 256), 256)
            total = gi_acc[r] if last else jnp.zeros((256, tok_rows), F32)
            for p in range(low, high, 2):
                pairs = jnp.concatenate([comb[p], comb[p + 1]], axis=1)
                if p < HEADS:
                    weight = wq[part, p * HEAD_DIM : (p + 2) * HEAD_DIM]
                else:
                    weight = wkv[part, (p - HEADS) * HEAD_DIM : (p + 2 - HEADS) * HEAD_DIM]
                total = total + dot(weight, pairs, NT)
            if last:
                gi_ref[:, part] = total.T.astype(BF)
            else:
                gi_acc[r] = total

    early = [s for s in range(slots) if ready(s) < 2]
    late = [s for s in range(slots) if ready(s) == 2]
    order = early + late
    grad_in(0, HEADS, False)
    finish_keyval()
    grad_in(HEADS, COLUMNS, True)
    for (k, half), copy in tok_copies.items():
        if not relayed or (k, half) not in ((1, 0), (2, 1)):
            copy.wait_recv()
    for i in range(slots + 1):
        if i < slots:
            multiply(order[i])
        if i > 0:
            spread(order[i - 1])
    for s in order:
        collect(s)
    for name, copy in copies.items():
        if name[0] == "fin":
            copy.wait_recv()
    for j in range(COLUMNS):
        if j < HEADS:
            gwq_ref[:, j * HEAD_DIM : (j + 1) * HEAD_DIM] = gath[j]
        else:
            gwkv_ref[:, (j - HEADS) * HEAD_DIM : (j - HEADS + 1) * HEAD_DIM] = gath[j]
    for copy in list(copies.values()) + list(tok_copies.values()):
        copy.wait_send()
    for one, two in halo_copies:
        @pl.when(ctx + 1 < n_ctx)
        def _():
            one.wait_send()

        @pl.when(ctx + 2 < n_ctx)
        def _():
            two.wait_send()

    for one, two in gh_copies:
        @pl.when(ctx >= 1)
        def _():
            one.wait_send()

        @pl.when(ctx >= 2)
        def _():
            two.wait_send()


def square_kernel(
    n_ctx,
    tok_hbm, seg_hbm, wq_hbm, wkv_hbm, do_hbm,
    ctx_ref, gi_ref, gwq_ref, gwkv_ref,
    tok, seg_ref, wq, wkv, do, tok_own, tok_in, q, kv_all, flip_all, ids_col, bias_ref, gkv, ghalo_out, ghalo_in,
    comb, comb_in, pair_out, pair_in, part_own, half_out, half_in, z_out, z_in, gath, gi_acc,
    load_s, tok_s, tok_r, halo_s, halo_r, gh_s, gh_r, comb_s, comb_r,
    pair_s, pair_r, half_s, half_r, z_s, z_r, fin_s, fin_r,
):
    n_z = n_ctx // 2
    n_h = n_z // 2
    tok_rows, model = tok.shape
    blocks = tok_rows // BLOCK
    dp = lax.axis_index("dp")
    ctx = lax.axis_index("ctx")
    core = lax.rem(ctx, 2)
    mate = ctx + 1 - 2 * core
    other = lax.rem(ctx + 2 * core - 1 + n_ctx, n_ctx)
    level = ctx // 2
    rows = gwq_ref.shape[0]
    part = rows // 2
    fast, slow = dp % 2, dp // 2
    place = ((fast, slow), (slow, fast))
    peers = (dp + 1 - 2 * fast, dp + 2 - 4 * slow, 3 - dp)
    top_half = level < n_h
    own_first = jnp.where(top_half, fast, slow)
    own_second = jnp.where(top_half, slow, fast)

    slots = [(0, 2), (4, 2), (8, 2), (HEADS, 1), (HEADS + 2, 1)]
    offsets = [0, 2, 4, 6, 7]
    direct = (2, 4)

    def z_peer(k):
        return lax.rem(level + k, n_z)

    def remote(src, dst, send, recv, to_dp, to_ctx):
        return pltpu.make_async_remote_copy(
            src_ref=src, dst_ref=dst, send_sem=send, recv_sem=recv,
            device_id=(to_dp, to_ctx), device_id_type=MESH,
        )

    barrier = pltpu.get_barrier_semaphore()
    for peer in peers:
        pl.semaphore_signal(barrier, inc=1, device_id=(peer, ctx), device_id_type=MESH)
    for k in range(1, n_z):
        pl.semaphore_signal(
            barrier, inc=1, device_id=(dp, 2 * z_peer(k) + core), device_id_type=MESH
        )
    for to in (mate, other):
        pl.semaphore_signal(barrier, inc=1, device_id=(dp, to), device_id_type=MESH)

    loads = [
        pltpu.make_async_copy(src, dst, load_s.at[i])
        for i, (src, dst) in enumerate(
            [(tok_hbm, tok), (wkv_hbm, wkv), (wq_hbm, wq), (do_hbm, do), (seg_hbm, seg_ref)]
        )
    ]
    for copy in loads:
        copy.start()

    @pl.when(ctx < 1)
    def _():
        kv_all[BLOCK:HALO, :] = jnp.zeros((HALO - BLOCK, kv_all.shape[1]), BF)

    @pl.when(ctx < 2)
    def _():
        kv_all[0:BLOCK, :] = jnp.zeros((BLOCK, kv_all.shape[1]), BF)

    @pl.when(ctx >= n_ctx - 1)
    def _():
        ghalo_in[BLOCK:HALO, :] = jnp.zeros((HALO - BLOCK, kv_all.shape[1]), BF)

    @pl.when(ctx >= n_ctx - 2)
    def _():
        ghalo_in[0:BLOCK, :] = jnp.zeros((BLOCK, kv_all.shape[1]), BF)

    loads[0].wait()
    tok_copies = [
        remote(tok_own.at[r], tok_in.at[r], tok_s.at[r], tok_r.at[r], peers[r], ctx) for r in range(2)
    ]
    chunks = model // BLOCK
    for c in range(chunks):
        flipped = tok[:, c * BLOCK : (c + 1) * BLOCK].T
        at = c * BLOCK
        while at < (c + 1) * BLOCK:
            shard = at // rows
            upto = min((shard + 1) * rows, (c + 1) * BLOCK)
            z = shard // 2
            low = (z % n_h) * rows + at - shard * rows
            tok_own[z // n_h, shard % 2, low : low + upto - at, :] = flipped[at - c * BLOCK : upto - c * BLOCK]
            at = upto
        if c == chunks // 2 - 1:
            pl.semaphore_wait(barrier, 4 + n_z)
            tok_copies[0].start()
    tok_copies[1].start()
    loads[1].wait()
    kv_all[HALO:, :] = dot(tok[...], wkv[...]).astype(BF)

    halo_copies = []
    for g in range(KV_HEADS):
        for i, piece in enumerate((g, KV_HEADS + g)):
            c = slice(piece * HEAD_DIM, (piece + 1) * HEAD_DIM)
            one = remote(kv_all.at[HALO:, c], kv_all.at[BLOCK:HALO, c], halo_s.at[g, i, 0],
                         halo_r.at[g, i, 0], dp, lax.rem(ctx + 1, n_ctx))
            two = remote(kv_all.at[HALO + BLOCK :, c], kv_all.at[0:BLOCK, c], halo_s.at[g, i, 1],
                         halo_r.at[g, i, 1], dp, lax.rem(ctx + 2, n_ctx))
            halo_copies.append((one, two))

    def start_halo(g):
        for one, _ in halo_copies[2 * g : 2 * g + 2]:
            @pl.when(ctx + 1 < n_ctx)
            def _():
                one.start()

        for _, two in halo_copies[2 * g : 2 * g + 2]:
            @pl.when(ctx + 2 < n_ctx)
            def _():
                two.start()

    start_halo(0)
    start_halo(1)

    loads[4].wait()
    tile0 = ctx * blocks - HALO // BLOCK
    for t in range(HALO // BLOCK + blocks):
        tile = tile0 + t
        start = pl.multiple_of(jnp.maximum(tile, 0) * BLOCK, BLOCK)
        row = seg_ref[0:1, pl.ds(start, BLOCK)]
        col = jnp.broadcast_to(row, (BLOCK, BLOCK)).T
        ids_col[t * BLOCK : (t + 1) * BLOCK, :] = jnp.where(tile < 0, -1, col)
    key_row = lax.broadcasted_iota(jnp.int32, (WINDOW, BLOCK), 0)
    query_col = lax.broadcasted_iota(jnp.int32, (WINDOW, BLOCK), 1)
    for b in range(blocks):
        first = pl.multiple_of(ctx * tok_rows + b * BLOCK, BLOCK)
        same = ids_col[b * BLOCK : b * BLOCK + WINDOW, :] == seg_ref[0:1, pl.ds(first, BLOCK)]
        bias_ref[b] = jnp.where((key_row <= query_col + HALO) & same, 0.0, -1e30)

    gkv[...] = jnp.zeros_like(gkv)
    loads[2].wait()
    for p in range(HEADS // 2):
        both = dot(tok[...], wq[:, 2 * p * HEAD_DIM : 2 * (p + 1) * HEAD_DIM]).astype(BF)
        q[2 * p] = both[:, :HEAD_DIM]
        q[2 * p + 1] = both[:, HEAD_DIM:]
    loads[3].wait()

    def columns(g):
        return [slice(j * HEAD_DIM, (j + 1) * HEAD_DIM) for j in (g, KV_HEADS + g)]

    def views(unit):
        g, p, b = unit
        window = slice(b * BLOCK, b * BLOCK + WINDOW)
        block = slice(b * BLOCK, b * BLOCK + BLOCK)
        kcol, vcol = columns(g)
        h = g * GROUP + 2 * p
        cols = [slice((h + i) * HEAD_DIM, (h + i + 1) * HEAD_DIM) for i in range(2)]
        return window, block, kcol, vcol, h, cols

    def score(unit):
        window, block, kcol, _, h, cols = views(unit)
        query = jnp.concatenate([q[h, block, :], q[h + 1, block, :]], axis=0)
        grad = jnp.concatenate([do[block, c] for c in cols], axis=0)
        bias = bias_ref[unit[2]]
        masked = dot(kv_all[window, kcol], query, NT) * SCALE + jnp.concatenate([bias, bias], axis=1)
        return query, grad, masked

    def soften(unit, query, grad, masked):
        window, _, _, vcol, _, _ = views(unit)
        expo = jnp.exp(masked - jnp.max(masked, axis=0, keepdims=True))
        inverse = 1.0 / jnp.sum(expo, axis=0, keepdims=True)
        probs_low = (expo * inverse).astype(BF)
        out_t = dot(flip_all[unit[0], 1, :, window], probs_low).astype(BF).astype(F32)
        grad_probs = dot(kv_all[window, vcol], grad, NT)
        return query, grad, expo, inverse, probs_low, out_t, grad_probs

    def derive(unit, query, grad, expo, inverse, probs_low, out_t, grad_probs):
        window, block, kcol, vcol, h, cols = views(unit)
        delta = jnp.sum(out_t * grad.astype(F32).T, axis=0, keepdims=True)
        grad_scores = (expo * ((grad_probs - delta) * (inverse * SCALE))).astype(BF)
        grad_query = dot(flip_all[unit[0], 0, :, window], grad_scores).T.astype(BF)
        out = out_t.T.astype(BF)
        for i, c in enumerate(cols):
            ctx_ref[block, c] = out[i * BLOCK : (i + 1) * BLOCK]
            comb[h + i, block, :] = grad_query[i * BLOCK : (i + 1) * BLOCK]
        gkv[window, kcol] += dot(grad_scores, query)
        gkv[window, vcol] += dot(probs_low, grad)

    copies = {}

    def near_halo(g):
        for i, c in enumerate(columns(g)):
            flip_all[g, i, :, HALO:] = kv_all[HALO:, c].T
        for one, _ in halo_copies[2 * g : 2 * g + 2]:
            @pl.when(ctx >= 1)
            def _():
                one.wait_recv()

        for i, c in enumerate(columns(g)):
            flip_all[g, i, :, BLOCK:HALO] = kv_all[BLOCK:HALO, c].T

    def far_halo(g):
        for _, two in halo_copies[2 * g : 2 * g + 2]:
            @pl.when(ctx >= 2)
            def _():
                two.wait_recv()

        for i, c in enumerate(columns(g)):
            flip_all[g, i, :, 0:BLOCK] = kv_all[0:BLOCK, c].T

    gh_copies = {}

    def send_halo(g):
        gh_copies[g] = []
        for i, c in enumerate(columns(g)):
            ghalo_out[:, c] = gkv[0:HALO, c].astype(BF)
            one = remote(ghalo_out.at[BLOCK:HALO, c], ghalo_in.at[BLOCK:HALO, c],
                         gh_s.at[g, i, 0], gh_r.at[g, i, 0], dp, lax.rem(ctx + n_ctx - 1, n_ctx))
            two = remote(ghalo_out.at[0:BLOCK, c], ghalo_in.at[0:BLOCK, c],
                         gh_s.at[g, i, 1], gh_r.at[g, i, 1], dp, lax.rem(ctx + n_ctx - 2, n_ctx))
            gh_copies[g].append((one, two))

            @pl.when(ctx >= 2)
            def _():
                two.start()

            @pl.when(ctx >= 1)
            def _():
                one.start()

    def finish_keyval(g):
        for one, two in gh_copies[g]:
            @pl.when(ctx + 1 < n_ctx)
            def _():
                one.wait_recv()

            @pl.when(ctx + 2 < n_ctx)
            def _():
                two.wait_recv()

        for i, c in enumerate(columns(g)):
            near = gkv[HALO:, c] + ghalo_in[BLOCK:HALO, c].astype(F32)
            at = HEADS + 2 * g + i
            comb[at, 0:BLOCK, :] = near[0:BLOCK].astype(BF)
            comb[at, BLOCK:, :] = (near[BLOCK:] + ghalo_in[0:BLOCK, c].astype(F32)).astype(BF)

    def send_slot(s):
        (low, width), at = slots[s], offsets[s]
        for r in range(2):
            theirs = pl.ds(low + width * (1 - place[r][0]), width)
            copy = remote(comb.at[theirs], comb_in.at[r, at : at + width], comb_s.at[s, r], comb_r.at[s, r],
                          peers[r], ctx)
            copy.start()
            copies["comb", s, r] = copy

    def multiply(s):
        (low, width), at = slots[s], offsets[s]
        for r in range(2):
            copies["comb", s, r].wait_recv()

        def product(r, parity):
            mine = [comb[low + width * place[r][0] + i] for i in range(width)]
            theirs = [comb_in[r, at + i] for i in range(width)]
            total = dot(tok_own[r, parity], jnp.concatenate(mine, axis=1))
            total = total + dot(tok_in[r, parity], jnp.concatenate(theirs, axis=1))
            return [total[:, i * HEAD_DIM : (i + 1) * HEAD_DIM] for i in range(width)]

        for r in range(2):
            for i, piece in enumerate(product(r, 1 - core)):
                pair_out[at + i, r] = piece.astype(BF)
        copy = remote(pair_out.at[at : at + width], pair_in.at[at : at + width], pair_s.at[s], pair_r.at[s],
                      dp, mate)
        copy.start()
        copies["pair", s] = copy
        for r in range(2):
            for i, piece in enumerate(product(r, core)):
                part_own[at + i, r] = piece

    def halve(s):
        (_, width), at = slots[s], offsets[s]
        copies["pair", s].wait_recv()
        for r in range(2):
            for i in range(at, at + width):
                for z in range(n_h):
                    away = pl.ds(pl.multiple_of(z * rows + (1 - place[r][1]) * part, 16), part)
                    total = part_own[i, r, away] + pair_in[i, r, away].astype(F32)
                    half_out[r, i, z] = total.astype(BF)
            copy = remote(half_out.at[r, at : at + width], half_in.at[r, at : at + width], half_s.at[s, r],
                          half_r.at[s, r], peers[1 - r], ctx)
            copy.start()
            copies["half", s, r] = copy

    def spread(s):
        (_, width), at = slots[s], offsets[s]
        for r in range(2):
            copies["half", s, r].wait_recv()
        for r in range(2):
            for z in range(n_h):
                for i in range(at, at + width):
                    here = pl.ds(pl.multiple_of(z * rows + place[r][1] * part, 16), part)
                    total = part_own[i, r, here] + pair_in[i, r, here].astype(F32)
                    total = total + half_in[r, i, z].astype(F32)
                    z_out[r * n_h + z, i] = total.astype(BF)
        for k in range(1, n_z):
            copy = remote(z_out.at[z_peer(k), at : at + width], z_in.at[k - 1, at : at + width],
                          z_s.at[s, k - 1], z_r.at[s, k - 1], dp, 2 * z_peer(k) + core)
            copy.start()
            copies["z", s, k] = copy

    def collect(s):
        (low, width), at = slots[s], offsets[s]
        r, z = level // n_h, lax.rem(level, n_h)
        here = pl.ds(pl.multiple_of(z * rows + own_second * part, 16), part)
        totals = [
            part_own[i, r, here] + pair_in[i, r, here].astype(F32) + half_in[r, i, z].astype(F32)
            for i in range(at, at + width)
        ]
        for k in range(1, n_z):
            copies["z", s, k].wait_recv()
            totals = [total + z_in[k - 1, at + i].astype(F32) for i, total in enumerate(totals)]
        spot = pl.ds(pl.multiple_of(own_second * part, 16), part)
        for i, total in enumerate(totals):
            gath[low + width * own_first + i, spot, :] = total.astype(BF)
        held = gath.at[pl.ds(low + width * own_first, width), spot, :]
        for k, peer in enumerate(peers if s in direct else peers[:2]):
            hand_on(s, k, held, peer)

    def hand_on(s, k, held, peer):
        copy = remote(held, held, fin_s.at[s, k], fin_r.at[s, k], peer, ctx)
        copy.start()
        copies["fin", s, k] = copy

    def relay(s):
        low, width = slots[s]
        for k, (flip_fast, flip_slow) in enumerate(((1, 0), (0, 1))):
            copies["fin", s, k].wait_recv()
            their_fast = fast + flip_fast * (1 - 2 * fast)
            their_slow = slow + flip_slow * (1 - 2 * slow)
            first = jnp.where(top_half, their_fast, their_slow)
            second = jnp.where(top_half, their_slow, their_fast)
            if width == 2:
                held = gath.at[pl.ds(low + width * first + k, 1), pl.ds(pl.multiple_of(second * part, 16), part), :]
            else:
                spot = pl.ds(pl.multiple_of(second * part + k * (part // 2), 16), part // 2)
                held = gath.at[pl.ds(low + width * first, 1), spot, :]
            hand_on(s, 2 + k, held, peers[1 - k])

    def grad_in(r, low, high, last):
        rows_in = slice(r * 256, (r + 1) * 256)
        total = gi_acc[r] if low else jnp.zeros((256, tok_rows), F32)
        for p in range(low, high, 2):
            pairs = jnp.concatenate([comb[p], comb[p + 1]], axis=1)
            if p < HEADS:
                weight = wq[rows_in, p * HEAD_DIM : (p + 2) * HEAD_DIM]
            else:
                weight = jnp.concatenate([wkv[rows_in, c] for c in columns((p - HEADS) // 2)], axis=1)
            total = total + dot(weight, pairs, NT)
        if last:
            gi_ref[:, rows_in] = total.T.astype(BF)
        else:
            gi_acc[r] = total

    def tokens_in():
        for copy in tok_copies:
            copy.wait_recv()

    def grad_in_heads(r):
        grad_in(r, 0, HEADS, False)

    def grad_in_rest():
        for r in range(model // 256):
            grad_in(r, HEADS, COLUMNS, True)

    units = [(g, p, b) for g in range(KV_HEADS) for p in range(GROUP // 2) for b in reversed(range(blocks))]
    before = {(g, 0, b): step for g in range(KV_HEADS) for b, step in ((blocks - 1, near_halo), (0, far_halo))}
    after = {
        (0, 1, 0): ((send_slot, 0),),
        (0, 2, 0): ((send_halo, 0),),
        (1, 0, 0): ((send_slot, 1),),
    }
    scored, softened = {}, {}
    for t in range(len(units) + 2):
        if t < len(units):
            if units[t] in before:
                before[units[t]](units[t][0])
            scored[t] = score(units[t])
        if 0 <= t - 1 < len(units):
            softened[t - 1] = soften(units[t - 1], *scored.pop(t - 1))
        if t >= 2:
            derive(units[t - 2], *softened.pop(t - 2))
            for step, *operands in after.get(units[t - 2], ()):
                step(*operands)
    schedule = (
        (send_halo, 1), (tokens_in,), (multiply, 0), (finish_keyval, 0), (send_slot, 3), (halve, 0), (send_slot, 2),
        (multiply, 1), (grad_in_heads, 0), (halve, 1), (spread, 0), (multiply, 3), (finish_keyval, 1),
        (send_slot, 4), (halve, 3), (grad_in_heads, 1), (grad_in_heads, 2), (multiply, 2), (spread, 1),
        (halve, 2), (multiply, 4), (collect, 0), (grad_in_heads, 3), (halve, 4), (spread, 3), (collect, 1),
        (grad_in_heads, 4), (relay, 0), (spread, 2), (spread, 4), (grad_in_heads, 5), (relay, 1), (collect, 3),
        (grad_in_rest,), (relay, 3), (collect, 2), (collect, 4),
    )
    for step, *operands in schedule:
        step(*operands)
    for name, copy in copies.items():
        if name[0] == "fin" and (name[1] in direct or name[2] >= 2):
            copy.wait_recv()
    for j in range(COLUMNS):
        if j < HEADS:
            gwq_ref[:, j * HEAD_DIM : (j + 1) * HEAD_DIM] = gath[j]
        else:
            at = KV_HEADS * ((j - HEADS) % 2) + (j - HEADS) // 2
            gwkv_ref[:, at * HEAD_DIM : (at + 1) * HEAD_DIM] = gath[j]
    for copy in list(copies.values()) + tok_copies:
        copy.wait_send()
    for one, two in halo_copies:
        @pl.when(ctx + 1 < n_ctx)
        def _():
            one.wait_send()

        @pl.when(ctx + 2 < n_ctx)
        def _():
            two.wait_send()

    for g in range(KV_HEADS):
        for one, two in gh_copies[g]:
            @pl.when(ctx >= 1)
            def _():
                one.wait_send()

            @pl.when(ctx >= 2)
            def _():
                two.wait_send()


def copy_kernel(*refs):
    count = (len(refs) - 1) // 2
    sources, targets, sems = refs[:count], refs[count : 2 * count], refs[-1]
    leave = [pltpu.make_async_copy(sources[i], targets[i], sems.at[i]) for i in range(count)]
    for copy in leave:
        copy.start()
    for copy in leave:
        copy.wait()


def copied(arrays):
    hbm = pl.BlockSpec(memory_space=pltpu.MemorySpace.HBM)
    return pl.pallas_call(
        copy_kernel,
        out_shape=tuple(jax.ShapeDtypeStruct(a.shape, a.dtype) for a in arrays),
        in_specs=[pl.BlockSpec(memory_space=pl.ANY)] * len(arrays),
        out_specs=(hbm,) * len(arrays),
        scratch_shapes=[pltpu.SemaphoreType.DMA((len(arrays),))],
        compiler_params=pltpu.CompilerParams(vmem_limit_bytes=1024 * 1024),
        name="results",
    )(*arrays)


def square_scratch(n_ctx, tok_rows, model, kv_cols):
    n_z = n_ctx // 2
    n_h = n_z // 2
    rows = model // n_ctx
    part = rows // 2
    keys = HALO + tok_rows
    held = COLUMNS // 2
    dma = pltpu.SemaphoreType.DMA
    return [
        pltpu.VMEM((tok_rows, model), BF),
        pltpu.VMEM((1, n_ctx * tok_rows), jnp.int32),
        pltpu.VMEM((model, model), BF),
        pltpu.VMEM((model, kv_cols), BF),
        pltpu.VMEM((tok_rows, model), BF),
        pltpu.VMEM((2, 2, n_h * rows, tok_rows), BF),
        pltpu.VMEM((2, 2, n_h * rows, tok_rows), BF),
        pltpu.VMEM((HEADS, tok_rows, HEAD_DIM), BF),
        pltpu.VMEM((keys, kv_cols), BF),
        pltpu.VMEM((KV_HEADS, 2, HEAD_DIM, keys), BF),
        pltpu.VMEM((keys, BLOCK), jnp.int32),
        pltpu.VMEM((tok_rows // BLOCK, WINDOW, BLOCK), F32),
        pltpu.VMEM((keys, kv_cols), F32),
        pltpu.VMEM((HALO, kv_cols), BF),
        pltpu.VMEM((HALO, kv_cols), BF),
        pltpu.VMEM((COLUMNS, tok_rows, HEAD_DIM), BF),
        pltpu.VMEM((2, held, tok_rows, HEAD_DIM), BF),
        pltpu.VMEM((held, 2, n_h * rows, HEAD_DIM), BF),
        pltpu.VMEM((held, 2, n_h * rows, HEAD_DIM), BF),
        pltpu.VMEM((held, 2, n_h * rows, HEAD_DIM), F32),
        pltpu.VMEM((2, held, n_h, part, HEAD_DIM), BF),
        pltpu.VMEM((2, held, n_h, part, HEAD_DIM), BF),
        pltpu.VMEM((n_z, held, part, HEAD_DIM), BF),
        pltpu.VMEM((n_z - 1, held, part, HEAD_DIM), BF),
        pltpu.VMEM((COLUMNS, rows, HEAD_DIM), BF),
        pltpu.VMEM((model // 256, 256, tok_rows), F32),
        dma((5,)),
        dma((2,)), dma((2,)),
        dma((KV_HEADS, 2, 2)), dma((KV_HEADS, 2, 2)),
        dma((KV_HEADS, 2, 2)), dma((KV_HEADS, 2, 2)),
        dma((5, 2)), dma((5, 2)),
        dma((5,)), dma((5,)),
        dma((5, 2)), dma((5, 2)),
        dma((5, n_z - 1)), dma((5, n_z - 1)),
        dma((5, 4)), dma((5, 4)),
    ]


def shards(tokens, segments, w_query, w_keyval, grad_context):
    hidden_in = tokens[0]
    tok_rows, model = hidden_in.shape
    kv_cols = w_keyval.shape[1]
    n_ctx = lax.axis_size("ctx")
    n_dp = lax.axis_size("dp")
    n_z = n_ctx // 2
    rows = model // n_ctx
    slots = COLUMNS // n_dp
    half = n_z * rows
    square = n_dp == 4 and n_ctx % 4 == 0 and rows % 32 == 0
    keys = HALO + tok_rows
    vmem = pl.BlockSpec(memory_space=pltpu.VMEM)
    hbm = pl.BlockSpec(memory_space=pltpu.MemorySpace.HBM)
    dma = pltpu.SemaphoreType.DMA
    results = pl.pallas_call(
        functools.partial(square_kernel, n_ctx) if square else functools.partial(layer_kernel, n_dp, n_ctx),
        out_shape=(
            pltpu.VMEM((tok_rows, model), BF),
            pltpu.VMEM((tok_rows, model), BF),
            pltpu.VMEM((rows, model), BF),
            pltpu.VMEM((rows, kv_cols), BF),
        ),
        in_specs=[hbm, hbm if square else vmem, hbm, hbm, hbm],
        out_specs=(vmem,) * 4,
        scratch_shapes=square_scratch(n_ctx, tok_rows, model, kv_cols) if square else [
            pltpu.VMEM((tok_rows, model), BF),
            pltpu.VMEM((model, model), BF),
            pltpu.VMEM((model, kv_cols), BF),
            pltpu.VMEM((tok_rows, model), BF),
            pltpu.VMEM((n_dp, 2, half, tok_rows), BF),
            pltpu.VMEM((HEADS, tok_rows, HEAD_DIM), BF),
            pltpu.VMEM((keys, kv_cols), BF),
            pltpu.VMEM((keys, BLOCK), jnp.int32),
            pltpu.VMEM((keys, kv_cols), F32),
            pltpu.VMEM((HALO, kv_cols), BF),
            pltpu.VMEM((HALO, kv_cols), BF),
            pltpu.VMEM((COLUMNS, tok_rows, HEAD_DIM), BF),
            pltpu.VMEM((slots, n_dp - 1, tok_rows, HEAD_DIM), BF),
            pltpu.VMEM((slots, half, HEAD_DIM), BF),
            pltpu.VMEM((slots, half, HEAD_DIM), BF),
            pltpu.VMEM((slots, half, HEAD_DIM), F32),
            pltpu.VMEM((slots, half, HEAD_DIM), BF),
            pltpu.VMEM((slots, n_z - 1, rows, HEAD_DIM), BF),
            pltpu.VMEM((COLUMNS, rows, HEAD_DIM), BF),
            pltpu.VMEM((model // 256, 256, tok_rows), F32),
            dma((4,)),
            dma((n_dp - 1, 2)), dma((n_dp - 1, 2)),
            dma((KV_HEADS, 2, 2)), dma((KV_HEADS, 2, 2)),
            dma((KV_HEADS, 2, 2)), dma((KV_HEADS, 2, 2)),
            dma((slots, n_dp - 1)), dma((slots, n_dp - 1)),
            dma((slots,)), dma((slots,)),
            dma((slots, n_z - 1)), dma((slots, n_z - 1)),
            dma((slots, n_dp - 1)), dma((slots, n_dp - 1)),
        ],
        compiler_params=pltpu.CompilerParams(
            collective_id=0, has_side_effects=True, vmem_limit_bytes=61 * 1024 * 1024
        ),
        name="layer",
    )(hidden_in, segments, w_query, w_keyval, grad_context[0])
    context, grad_in, grad_wq, grad_wkv = copied(results)
    return context[None], grad_in[None], grad_wq, grad_wkv


def solution(mesh):
    placed = (P("dp", "ctx", None), P("dp", None), P(), P(), P("dp", "ctx", None))
    return jax.shard_map(
        shards,
        mesh=mesh,
        in_specs=placed,
        out_specs=(P("dp", "ctx", None), P("dp", "ctx", None), P("ctx", None), P("ctx", None)),
        check_vma=False,
    )
```

```python
import functools

import jax
import jax.numpy as jnp
from jax import lax
from jax.experimental import pallas as pl
from jax.experimental.pallas import tpu as pltpu
from jax.sharding import PartitionSpec as P

HEADS = 12
KV_HEADS = 2
HEAD_DIM = 128
WINDOW = 512
BLOCK = 128
HALO = WINDOW - BLOCK
GROUP = HEADS // KV_HEADS
COLUMNS = HEADS + 2 * KV_HEADS
SCALE = HEAD_DIM ** (-0.5)
MESH = pl.DeviceIdType.MESH
NT = (((1,), (1,)), ((), ()))
NN = (((1,), (0,)), ((), ()))
BF = jnp.bfloat16
F32 = jnp.float32


def dot(a, b, dims=NN):
    return lax.dot_general(a, b, dims, preferred_element_type=F32)


def layer_kernel(
    n_dp, n_ctx,
    tok_hbm, seg_ref, wq_hbm, wkv_hbm, do_hbm,
    ctx_ref, gi_ref, gwq_ref, gwkv_ref,
    tok, wq, wkv, do, tok_all, q, kv_all, ids_col, gkv, ghalo_out, ghalo_in, comb, comb_in,
    pair_out, pair_in, part_own, z_out, z_in, gath, gi_acc,
    load_s, tok_s, tok_r, halo_s, halo_r, gh_s, gh_r, comb_s, comb_r,
    pair_s, pair_r, z_s, z_r, fin_s, fin_r,
):
    n_z = n_ctx // 2
    slots = COLUMNS // n_dp
    tok_rows, model = tok.shape
    dp = lax.axis_index("dp")
    ctx = lax.axis_index("ctx")
    core = lax.rem(ctx, 2)
    mate = ctx + 1 - 2 * core
    other = lax.rem(ctx + 2 * core - 1 + n_ctx, n_ctx)
    level = ctx // 2
    rows = gwq_ref.shape[0]

    relayed = n_dp == 4

    def dp_peer(k):
        if relayed:
            return (dp + 1 - 2 * (dp % 2), dp + 2 - 4 * (dp // 2), 3 - dp)[k - 1]
        return lax.rem(dp + k, n_dp)

    def z_peer(k):
        return lax.rem(level + k, n_z)

    def remote(src, dst, send, recv, to_dp, to_ctx):
        return pltpu.make_async_remote_copy(
            src_ref=src, dst_ref=dst, send_sem=send, recv_sem=recv,
            device_id=(to_dp, to_ctx), device_id_type=MESH,
        )

    barrier = pltpu.get_barrier_semaphore()
    for k in range(1, n_dp):
        pl.semaphore_signal(barrier, inc=1, device_id=(dp_peer(k), ctx), device_id_type=MESH)
    for k in range(1, n_z):
        pl.semaphore_signal(
            barrier, inc=1, device_id=(dp, 2 * z_peer(k) + core), device_id_type=MESH
        )
    for to in (mate, other):
        pl.semaphore_signal(barrier, inc=1, device_id=(dp, to), device_id_type=MESH)

    loads = [
        pltpu.make_async_copy(src, dst, load_s.at[i])
        for i, (src, dst) in enumerate(
            [(tok_hbm, tok), (wkv_hbm, wkv), (wq_hbm, wq), (do_hbm, do)]
        )
    ]
    for copy in loads:
        copy.start()

    tile0 = ctx * (tok_rows // BLOCK) - HALO // BLOCK
    for t in range((HALO + tok_rows) // BLOCK):
        tile = tile0 + t
        start = pl.multiple_of(jnp.maximum(tile, 0) * BLOCK, BLOCK)
        row = seg_ref[0:1, pl.ds(start, BLOCK)]
        col = jnp.broadcast_to(row, (BLOCK, BLOCK)).T
        ids_col[t * BLOCK : (t + 1) * BLOCK, :] = jnp.where(tile < 0, -1, col)

    @pl.when(ctx < 1)
    def _():
        kv_all[BLOCK:HALO, :] = jnp.zeros((HALO - BLOCK, kv_all.shape[1]), BF)

    @pl.when(ctx < 2)
    def _():
        kv_all[0:BLOCK, :] = jnp.zeros((BLOCK, kv_all.shape[1]), BF)

    @pl.when(ctx >= n_ctx - 1)
    def _():
        ghalo_in[BLOCK:HALO, :] = jnp.zeros((HALO - BLOCK, kv_all.shape[1]), BF)

    @pl.when(ctx >= n_ctx - 2)
    def _():
        ghalo_in[0:BLOCK, :] = jnp.zeros((BLOCK, kv_all.shape[1]), BF)

    gkv[...] = jnp.zeros_like(gkv)
    loads[0].wait()
    for c in range(model // BLOCK):
        flipped = tok[:, c * BLOCK : (c + 1) * BLOCK].T
        at = c * BLOCK
        while at < (c + 1) * BLOCK:
            shard = at // rows
            upto = min((shard + 1) * rows, (c + 1) * BLOCK)
            low = (shard // 2) * rows + at - shard * rows
            tok_all[0, shard % 2, low : low + upto - at, :] = flipped[at - c * BLOCK : upto - c * BLOCK]
            at = upto

    loads[1].wait()
    kv_all[HALO:, :] = dot(tok[...], wkv[...]).astype(BF)
    pl.semaphore_wait(barrier, n_dp + n_z)

    def tok_copy(origin, slot, k, half):
        return remote(tok_all.at[origin, half], tok_all.at[slot, half], tok_s.at[slot - 1, half],
                      tok_r.at[slot - 1, half], dp_peer(k), ctx)

    tok_copies = {}
    for i in range(2):
        for k in range(1, 3 if relayed else n_dp):
            half = (i + k + 1) % 2
            tok_copies[k, half] = tok_copy(0, k, k, half)
            tok_copies[k, half].start()

    halo_copies = []
    for g in range(KV_HEADS):
        for i, part in enumerate((g, KV_HEADS + g)):
            c = slice(part * HEAD_DIM, (part + 1) * HEAD_DIM)
            one = remote(kv_all.at[HALO:, c], kv_all.at[BLOCK:HALO, c], halo_s.at[g, i, 0],
                         halo_r.at[g, i, 0], dp, lax.rem(ctx + 1, n_ctx))
            two = remote(kv_all.at[HALO + BLOCK :, c], kv_all.at[0:BLOCK, c], halo_s.at[g, i, 1],
                         halo_r.at[g, i, 1], dp, lax.rem(ctx + 2, n_ctx))
            halo_copies.append((one, two))

            @pl.when(ctx + 2 < n_ctx)
            def _():
                two.start()

            @pl.when(ctx + 1 < n_ctx)
            def _():
                one.start()

    loads[2].wait()
    for p in range(HEADS // 2):
        both = dot(tok[...], wq[:, 2 * p * HEAD_DIM : 2 * (p + 1) * HEAD_DIM]).astype(BF)
        q[2 * p] = both[:, :HEAD_DIM]
        q[2 * p + 1] = both[:, HEAD_DIM:]
    loads[3].wait()

    key_row = lax.broadcasted_iota(jnp.int32, (WINDOW, BLOCK), 0)
    query_col = lax.broadcasted_iota(jnp.int32, (WINDOW, BLOCK), 1)

    def attend(g, b):
        row0 = pl.multiple_of(b * BLOCK, BLOCK)
        kcol = slice(g * HEAD_DIM, (g + 1) * HEAD_DIM)
        vcol = slice((KV_HEADS + g) * HEAD_DIM, (KV_HEADS + g + 1) * HEAD_DIM)
        window = pl.ds(row0, WINDOW)
        block = pl.ds(row0, BLOCK)
        keys = kv_all[window, kcol]
        vals = kv_all[window, vcol]
        keys_t = keys.T
        vals_t = vals.T
        first = pl.multiple_of(ctx * tok_rows + b * BLOCK, BLOCK)
        same = ids_col[window, :] == seg_ref[0:1, pl.ds(first, BLOCK)]
        bias = jnp.where((key_row <= query_col + HALO) & same, 0.0, -1e30)
        bias = jnp.concatenate([bias, bias], axis=1)
        grad_key = jnp.zeros((WINDOW, HEAD_DIM), F32)
        grad_val = jnp.zeros((WINDOW, HEAD_DIM), F32)
        for pair in range(GROUP // 2):
            h = g * GROUP + 2 * pair
            cols = [slice((h + i) * HEAD_DIM, (h + i + 1) * HEAD_DIM) for i in range(2)]
            query = jnp.concatenate([q[h, block, :], q[h + 1, block, :]], axis=0)
            grad = jnp.concatenate([do[block, c] for c in cols], axis=0)
            masked = jnp.where(bias < 0.0, -1e30, dot(keys, query, NT) * SCALE)
            top = jnp.max(masked, axis=0, keepdims=True)
            expo = jnp.exp(masked - top)
            probs = expo * (1.0 / jnp.sum(expo, axis=0, keepdims=True))
            probs_low = probs.astype(BF)
            out_t = dot(vals_t, probs_low).astype(BF).astype(F32)
            delta = jnp.sum(out_t * grad.astype(F32).T, axis=0, keepdims=True)
            grad_scores = (probs * (dot(vals, grad, NT) - delta) * SCALE).astype(BF)
            grad_query = dot(keys_t, grad_scores).T.astype(BF)
            out = out_t.T.astype(BF)
            for i, c in enumerate(cols):
                ctx_ref[block, c] = out[i * BLOCK : (i + 1) * BLOCK]
                comb[h + i, block, :] = grad_query[i * BLOCK : (i + 1) * BLOCK]
            grad_key = grad_key + dot(grad_scores, query)
            grad_val = grad_val + dot(probs_low, grad)
        gkv[window, kcol] += grad_key
        gkv[window, vcol] += grad_val

    copies = {}

    def send_slot(s):
        for k in range(1, n_dp):
            copy = remote(comb.at[s * n_dp + dp_peer(k)], comb_in.at[s, k - 1],
                          comb_s.at[s, k - 1], comb_r.at[s, k - 1], dp_peer(k), ctx)
            copy.start()
            copies["comb", s, k] = copy

    def ready(s):
        last = (s + 1) * n_dp
        return 0 if last <= GROUP else 1 if last <= HEADS else 2

    gh_copies = []
    for g in range(KV_HEADS):
        for one, two in halo_copies[2 * g : 2 * g + 2]:
            @pl.when(ctx >= 1)
            def _():
                one.wait_recv()

            @pl.when(ctx >= 2)
            def _():
                two.wait_recv()

        @pl.loop(0, tok_rows // BLOCK)
        def _(b):
            attend(g, b)

        for i, part in enumerate((g, KV_HEADS + g)):
            c = slice(part * HEAD_DIM, (part + 1) * HEAD_DIM)
            ghalo_out[:, c] = gkv[0:HALO, c].astype(BF)
            one = remote(ghalo_out.at[BLOCK:HALO, c], ghalo_in.at[BLOCK:HALO, c],
                         gh_s.at[g, i, 0], gh_r.at[g, i, 0], dp, lax.rem(ctx + n_ctx - 1, n_ctx))
            two = remote(ghalo_out.at[0:BLOCK, c], ghalo_in.at[0:BLOCK, c],
                         gh_s.at[g, i, 1], gh_r.at[g, i, 1], dp, lax.rem(ctx + n_ctx - 2, n_ctx))
            gh_copies.append((one, two))

            @pl.when(ctx >= 2)
            def _():
                two.start()

            @pl.when(ctx >= 1)
            def _():
                one.start()

        if g == 0 and relayed:
            tok_copies[1, 0].wait_recv()
            tok_copies[3, 0] = tok_copy(1, 3, 2, 0)
            tok_copies[3, 0].start()
            tok_copies[2, 1].wait_recv()
            tok_copies[3, 1] = tok_copy(2, 3, 1, 1)
            tok_copies[3, 1].start()

        for s in range(slots):
            if ready(s) == g:
                send_slot(s)

    def finish_keyval():
        for one, two in gh_copies:
            @pl.when(ctx + 1 < n_ctx)
            def _():
                one.wait_recv()

            @pl.when(ctx + 2 < n_ctx)
            def _():
                two.wait_recv()

        for part in range(2 * KV_HEADS):
            c = slice(part * HEAD_DIM, (part + 1) * HEAD_DIM)
            near = gkv[HALO:, c] + ghalo_in[BLOCK:HALO, c].astype(F32)
            comb[HEADS + part, 0:BLOCK, :] = near[0:BLOCK].astype(BF)
            comb[HEADS + part, BLOCK:, :] = (near[BLOCK:] + ghalo_in[0:BLOCK, c].astype(F32)).astype(BF)
        for s in range(slots):
            if ready(s) == 2:
                send_slot(s)

    def partial(s, parity):
        total = dot(tok_all[0, parity], comb[s * n_dp + dp])
        for k in range(1, n_dp):
            total = total + dot(tok_all[k, parity], comb_in[s, k - 1])
        return total

    def multiply(s):
        for k in range(1, n_dp):
            copies["comb", s, k].wait_recv()
        pair_out[s] = partial(s, 1 - core).astype(BF)
        copy = remote(pair_out.at[s], pair_in.at[s], pair_s.at[s], pair_r.at[s], dp, mate)
        copy.start()
        copies["pair", s] = copy
        part_own[s] = partial(s, core)

    def spread(s):
        copies["pair", s].wait_recv()
        z_out[s] = (part_own[s] + pair_in[s].astype(F32)).astype(BF)
        for k in range(1, n_z):
            piece = pl.ds(pl.multiple_of(z_peer(k) * rows, 16), rows)
            copy = remote(z_out.at[s, piece], z_in.at[s, k - 1], z_s.at[s, k - 1], z_r.at[s, k - 1],
                          dp, 2 * z_peer(k) + core)
            copy.start()
            copies["z", s, k] = copy

    def collect(s):
        mine = pl.ds(pl.multiple_of(level * rows, 16), rows)
        total = part_own[s, mine] + pair_in[s, mine].astype(F32)
        for k in range(1, n_z):
            copies["z", s, k].wait_recv()
            total = total + z_in[s, k - 1].astype(F32)
        spot = s * n_dp + dp
        gath[spot] = total.astype(BF)
        for k in range(1, n_dp):
            copy = remote(gath.at[spot], gath.at[spot], fin_s.at[s, k - 1], fin_r.at[s, k - 1],
                          dp_peer(k), ctx)
            copy.start()
            copies["fin", s, k] = copy

    def grad_in(low, high, last):
        @pl.loop(0, model // 256)
        def _(r):
            part = pl.ds(pl.multiple_of(r * 256, 256), 256)
            total = gi_acc[r] if last else jnp.zeros((256, tok_rows), F32)
            for p in range(low, high, 2):
                pairs = jnp.concatenate([comb[p], comb[p + 1]], axis=1)
                if p < HEADS:
                    weight = wq[part, p * HEAD_DIM : (p + 2) * HEAD_DIM]
                else:
                    weight = wkv[part, (p - HEADS) * HEAD_DIM : (p + 2 - HEADS) * HEAD_DIM]
                total = total + dot(weight, pairs, NT)
            if last:
                gi_ref[:, part] = total.T.astype(BF)
            else:
                gi_acc[r] = total

    early = [s for s in range(slots) if ready(s) < 2]
    late = [s for s in range(slots) if ready(s) == 2]
    order = early + late
    grad_in(0, HEADS, False)
    finish_keyval()
    grad_in(HEADS, COLUMNS, True)
    for (k, half), copy in tok_copies.items():
        if not relayed or (k, half) not in ((1, 0), (2, 1)):
            copy.wait_recv()
    for i in range(slots + 1):
        if i < slots:
            multiply(order[i])
        if i > 0:
            spread(order[i - 1])
    for s in order:
        collect(s)
    for name, copy in copies.items():
        if name[0] == "fin":
            copy.wait_recv()
    for j in range(COLUMNS):
        if j < HEADS:
            gwq_ref[:, j * HEAD_DIM : (j + 1) * HEAD_DIM] = gath[j]
        else:
            gwkv_ref[:, (j - HEADS) * HEAD_DIM : (j - HEADS + 1) * HEAD_DIM] = gath[j]
    for copy in list(copies.values()) + list(tok_copies.values()):
        copy.wait_send()
    for one, two in halo_copies:
        @pl.when(ctx + 1 < n_ctx)
        def _():
            one.wait_send()

        @pl.when(ctx + 2 < n_ctx)
        def _():
            two.wait_send()

    for one, two in gh_copies:
        @pl.when(ctx >= 1)
        def _():
            one.wait_send()

        @pl.when(ctx >= 2)
        def _():
            two.wait_send()


def square_kernel(
    n_ctx,
    tok_hbm, seg_hbm, wq_hbm, wkv_hbm, do_hbm,
    ctx_ref, gi_ref, gwq_ref, gwkv_ref,
    tok, seg_ref, wq, wkv, do, tok_own, tok_in, q, kv_all, flip_all, ids_col, bias_ref, gkv, ghalo_out, ghalo_in,
    comb, comb_in, pair_out, pair_in, part_own, half_out, half_in, z_out, z_in, gath, gi_acc,
    load_s, tok_s, tok_r, halo_s, halo_r, gh_s, gh_r, comb_s, comb_r,
    pair_s, pair_r, half_s, half_r, z_s, z_r, fin_s, fin_r,
):
    n_z = n_ctx // 2
    n_h = n_z // 2
    tok_rows, model = tok.shape
    blocks = tok_rows // BLOCK
    dp = lax.axis_index("dp")
    ctx = lax.axis_index("ctx")
    core = lax.rem(ctx, 2)
    mate = ctx + 1 - 2 * core
    other = lax.rem(ctx + 2 * core - 1 + n_ctx, n_ctx)
    level = ctx // 2
    rows = gwq_ref.shape[0]
    part = rows // 2
    fast, slow = dp % 2, dp // 2
    place = ((fast, slow), (slow, fast))
    peers = (dp + 1 - 2 * fast, dp + 2 - 4 * slow, 3 - dp)
    top_half = level < n_h
    own_first = jnp.where(top_half, fast, slow)
    own_second = jnp.where(top_half, slow, fast)

    slots = [(0, 2), (4, 2), (8, 2), (HEADS, 1), (HEADS + 2, 1)]
    offsets = [0, 2, 4, 6, 7]
    direct = (2, 4)

    def z_peer(k):
        return lax.rem(level + k, n_z)

    def remote(src, dst, send, recv, to_dp, to_ctx):
        return pltpu.make_async_remote_copy(
            src_ref=src, dst_ref=dst, send_sem=send, recv_sem=recv,
            device_id=(to_dp, to_ctx), device_id_type=MESH,
        )

    barrier = pltpu.get_barrier_semaphore()
    for peer in peers:
        pl.semaphore_signal(barrier, inc=1, device_id=(peer, ctx), device_id_type=MESH)
    for k in range(1, n_z):
        pl.semaphore_signal(
            barrier, inc=1, device_id=(dp, 2 * z_peer(k) + core), device_id_type=MESH
        )
    for to in (mate, other):
        pl.semaphore_signal(barrier, inc=1, device_id=(dp, to), device_id_type=MESH)

    loads = [
        pltpu.make_async_copy(src, dst, load_s.at[i])
        for i, (src, dst) in enumerate(
            [(tok_hbm, tok), (wkv_hbm, wkv), (wq_hbm, wq), (do_hbm, do), (seg_hbm, seg_ref)]
        )
    ]
    for copy in loads:
        copy.start()

    @pl.when(ctx < 1)
    def _():
        kv_all[BLOCK:HALO, :] = jnp.zeros((HALO - BLOCK, kv_all.shape[1]), BF)

    @pl.when(ctx < 2)
    def _():
        kv_all[0:BLOCK, :] = jnp.zeros((BLOCK, kv_all.shape[1]), BF)

    @pl.when(ctx >= n_ctx - 1)
    def _():
        ghalo_in[BLOCK:HALO, :] = jnp.zeros((HALO - BLOCK, kv_all.shape[1]), BF)

    @pl.when(ctx >= n_ctx - 2)
    def _():
        ghalo_in[0:BLOCK, :] = jnp.zeros((BLOCK, kv_all.shape[1]), BF)

    loads[0].wait()
    tok_copies = [
        remote(tok_own.at[r], tok_in.at[r], tok_s.at[r], tok_r.at[r], peers[r], ctx) for r in range(2)
    ]
    chunks = model // BLOCK
    for c in range(chunks):
        flipped = tok[:, c * BLOCK : (c + 1) * BLOCK].T
        at = c * BLOCK
        while at < (c + 1) * BLOCK:
            shard = at // rows
            upto = min((shard + 1) * rows, (c + 1) * BLOCK)
            z = shard // 2
            low = (z % n_h) * rows + at - shard * rows
            tok_own[z // n_h, shard % 2, low : low + upto - at, :] = flipped[at - c * BLOCK : upto - c * BLOCK]
            at = upto
        if c == chunks // 2 - 1:
            pl.semaphore_wait(barrier, 4 + n_z)
            tok_copies[0].start()
    tok_copies[1].start()
    loads[1].wait()
    kv_all[HALO:, :] = dot(tok[...], wkv[...]).astype(BF)

    halo_copies = []
    for g in range(KV_HEADS):
        for i, piece in enumerate((g, KV_HEADS + g)):
            c = slice(piece * HEAD_DIM, (piece + 1) * HEAD_DIM)
            one = remote(kv_all.at[HALO:, c], kv_all.at[BLOCK:HALO, c], halo_s.at[g, i, 0],
                         halo_r.at[g, i, 0], dp, lax.rem(ctx + 1, n_ctx))
            two = remote(kv_all.at[HALO + BLOCK :, c], kv_all.at[0:BLOCK, c], halo_s.at[g, i, 1],
                         halo_r.at[g, i, 1], dp, lax.rem(ctx + 2, n_ctx))
            halo_copies.append((one, two))

    def start_halo(g):
        for one, _ in halo_copies[2 * g : 2 * g + 2]:
            @pl.when(ctx + 1 < n_ctx)
            def _():
                one.start()

        for _, two in halo_copies[2 * g : 2 * g + 2]:
            @pl.when(ctx + 2 < n_ctx)
            def _():
                two.start()

    start_halo(0)
    start_halo(1)

    loads[4].wait()
    tile0 = ctx * blocks - HALO // BLOCK
    for t in range(HALO // BLOCK + blocks):
        tile = tile0 + t
        start = pl.multiple_of(jnp.maximum(tile, 0) * BLOCK, BLOCK)
        row = seg_ref[0:1, pl.ds(start, BLOCK)]
        col = jnp.broadcast_to(row, (BLOCK, BLOCK)).T
        ids_col[t * BLOCK : (t + 1) * BLOCK, :] = jnp.where(tile < 0, -1, col)
    key_row = lax.broadcasted_iota(jnp.int32, (WINDOW, BLOCK), 0)
    query_col = lax.broadcasted_iota(jnp.int32, (WINDOW, BLOCK), 1)
    for b in range(blocks):
        first = pl.multiple_of(ctx * tok_rows + b * BLOCK, BLOCK)
        same = ids_col[b * BLOCK : b * BLOCK + WINDOW, :] == seg_ref[0:1, pl.ds(first, BLOCK)]
        bias_ref[b] = jnp.where((key_row <= query_col + HALO) & same, 0.0, -1e30)

    gkv[...] = jnp.zeros_like(gkv)
    loads[2].wait()
    for p in range(HEADS // 2):
        both = dot(tok[...], wq[:, 2 * p * HEAD_DIM : 2 * (p + 1) * HEAD_DIM]).astype(BF)
        q[2 * p] = both[:, :HEAD_DIM]
        q[2 * p + 1] = both[:, HEAD_DIM:]
    loads[3].wait()

    def columns(g):
        return [slice(j * HEAD_DIM, (j + 1) * HEAD_DIM) for j in (g, KV_HEADS + g)]

    def views(unit):
        g, p, b = unit
        window = slice(b * BLOCK, b * BLOCK + WINDOW)
        block = slice(b * BLOCK, b * BLOCK + BLOCK)
        kcol, vcol = columns(g)
        h = g * GROUP + 2 * p
        cols = [slice((h + i) * HEAD_DIM, (h + i + 1) * HEAD_DIM) for i in range(2)]
        return window, block, kcol, vcol, h, cols

    def score(unit):
        window, block, kcol, _, h, cols = views(unit)
        query = jnp.concatenate([q[h, block, :], q[h + 1, block, :]], axis=0)
        grad = jnp.concatenate([do[block, c] for c in cols], axis=0)
        bias = bias_ref[unit[2]]
        masked = dot(kv_all[window, kcol], query, NT) * SCALE + jnp.concatenate([bias, bias], axis=1)
        return query, grad, masked

    def soften(unit, query, grad, masked):
        window, _, _, vcol, _, _ = views(unit)
        expo = jnp.exp(masked - jnp.max(masked, axis=0, keepdims=True))
        inverse = 1.0 / jnp.sum(expo, axis=0, keepdims=True)
        probs_low = (expo * inverse).astype(BF)
        out_t = dot(flip_all[unit[0], 1, :, window], probs_low).astype(BF).astype(F32)
        grad_probs = dot(kv_all[window, vcol], grad, NT)
        return query, grad, expo, inverse, probs_low, out_t, grad_probs

    def derive(unit, query, grad, expo, inverse, probs_low, out_t, grad_probs):
        window, block, kcol, vcol, h, cols = views(unit)
        delta = jnp.sum(out_t * grad.astype(F32).T, axis=0, keepdims=True)
        grad_scores = (expo * ((grad_probs - delta) * (inverse * SCALE))).astype(BF)
        grad_query = dot(flip_all[unit[0], 0, :, window], grad_scores).T.astype(BF)
        out = out_t.T.astype(BF)
        for i, c in enumerate(cols):
            ctx_ref[block, c] = out[i * BLOCK : (i + 1) * BLOCK]
            comb[h + i, block, :] = grad_query[i * BLOCK : (i + 1) * BLOCK]
        gkv[window, kcol] += dot(grad_scores, query)
        gkv[window, vcol] += dot(probs_low, grad)

    copies = {}

    def near_halo(g):
        for i, c in enumerate(columns(g)):
            flip_all[g, i, :, HALO:] = kv_all[HALO:, c].T
        for one, _ in halo_copies[2 * g : 2 * g + 2]:
            @pl.when(ctx >= 1)
            def _():
                one.wait_recv()

        for i, c in enumerate(columns(g)):
            flip_all[g, i, :, BLOCK:HALO] = kv_all[BLOCK:HALO, c].T

    def far_halo(g):
        for _, two in halo_copies[2 * g : 2 * g + 2]:
            @pl.when(ctx >= 2)
            def _():
                two.wait_recv()

        for i, c in enumerate(columns(g)):
            flip_all[g, i, :, 0:BLOCK] = kv_all[0:BLOCK, c].T

    gh_copies = {}

    def send_halo(g):
        gh_copies[g] = []
        for i, c in enumerate(columns(g)):
            ghalo_out[:, c] = gkv[0:HALO, c].astype(BF)
            one = remote(ghalo_out.at[BLOCK:HALO, c], ghalo_in.at[BLOCK:HALO, c],
                         gh_s.at[g, i, 0], gh_r.at[g, i, 0], dp, lax.rem(ctx + n_ctx - 1, n_ctx))
            two = remote(ghalo_out.at[0:BLOCK, c], ghalo_in.at[0:BLOCK, c],
                         gh_s.at[g, i, 1], gh_r.at[g, i, 1], dp, lax.rem(ctx + n_ctx - 2, n_ctx))
            gh_copies[g].append((one, two))

            @pl.when(ctx >= 2)
            def _():
                two.start()

            @pl.when(ctx >= 1)
            def _():
                one.start()

    def finish_keyval(g):
        for one, two in gh_copies[g]:
            @pl.when(ctx + 1 < n_ctx)
            def _():
                one.wait_recv()

            @pl.when(ctx + 2 < n_ctx)
            def _():
                two.wait_recv()

        for i, c in enumerate(columns(g)):
            near = gkv[HALO:, c] + ghalo_in[BLOCK:HALO, c].astype(F32)
            at = HEADS + 2 * g + i
            comb[at, 0:BLOCK, :] = near[0:BLOCK].astype(BF)
            comb[at, BLOCK:, :] = (near[BLOCK:] + ghalo_in[0:BLOCK, c].astype(F32)).astype(BF)

    def send_slot(s):
        (low, width), at = slots[s], offsets[s]
        for r in range(2):
            theirs = pl.ds(low + width * (1 - place[r][0]), width)
            copy = remote(comb.at[theirs], comb_in.at[r, at : at + width], comb_s.at[s, r], comb_r.at[s, r],
                          peers[r], ctx)
            copy.start()
            copies["comb", s, r] = copy

    def multiply(s):
        (low, width), at = slots[s], offsets[s]
        for r in range(2):
            copies["comb", s, r].wait_recv()

        def product(r, parity):
            mine = [comb[low + width * place[r][0] + i] for i in range(width)]
            theirs = [comb_in[r, at + i] for i in range(width)]
            total = dot(tok_own[r, parity], jnp.concatenate(mine, axis=1))
            total = total + dot(tok_in[r, parity], jnp.concatenate(theirs, axis=1))
            return [total[:, i * HEAD_DIM : (i + 1) * HEAD_DIM] for i in range(width)]

        for r in range(2):
            for i, piece in enumerate(product(r, 1 - core)):
                pair_out[at + i, r] = piece.astype(BF)
        copy = remote(pair_out.at[at : at + width], pair_in.at[at : at + width], pair_s.at[s], pair_r.at[s],
                      dp, mate)
        copy.start()
        copies["pair", s] = copy
        for r in range(2):
            for i, piece in enumerate(product(r, core)):
                part_own[at + i, r] = piece

    def halve(s):
        (_, width), at = slots[s], offsets[s]
        copies["pair", s].wait_recv()
        for r in range(2):
            for i in range(at, at + width):
                for z in range(n_h):
                    away = pl.ds(pl.multiple_of(z * rows + (1 - place[r][1]) * part, 16), part)
                    total = part_own[i, r, away] + pair_in[i, r, away].astype(F32)
                    half_out[r, i, z] = total.astype(BF)
            copy = remote(half_out.at[r, at : at + width], half_in.at[r, at : at + width], half_s.at[s, r],
                          half_r.at[s, r], peers[1 - r], ctx)
            copy.start()
            copies["half", s, r] = copy

    def spread(s):
        (_, width), at = slots[s], offsets[s]
        for r in range(2):
            copies["half", s, r].wait_recv()
        for r in range(2):
            for z in range(n_h):
                for i in range(at, at + width):
                    here = pl.ds(pl.multiple_of(z * rows + place[r][1] * part, 16), part)
                    total = part_own[i, r, here] + pair_in[i, r, here].astype(F32)
                    total = total + half_in[r, i, z].astype(F32)
                    z_out[r * n_h + z, i] = total.astype(BF)
        for k in range(1, n_z):
            copy = remote(z_out.at[z_peer(k), at : at + width], z_in.at[k - 1, at : at + width],
                          z_s.at[s, k - 1], z_r.at[s, k - 1], dp, 2 * z_peer(k) + core)
            copy.start()
            copies["z", s, k] = copy

    def collect(s):
        (low, width), at = slots[s], offsets[s]
        r, z = level // n_h, lax.rem(level, n_h)
        here = pl.ds(pl.multiple_of(z * rows + own_second * part, 16), part)
        totals = [
            part_own[i, r, here] + pair_in[i, r, here].astype(F32) + half_in[r, i, z].astype(F32)
            for i in range(at, at + width)
        ]
        for k in range(1, n_z):
            copies["z", s, k].wait_recv()
            totals = [total + z_in[k - 1, at + i].astype(F32) for i, total in enumerate(totals)]
        spot = pl.ds(pl.multiple_of(own_second * part, 16), part)
        for i, total in enumerate(totals):
            gath[low + width * own_first + i, spot, :] = total.astype(BF)
        held = gath.at[pl.ds(low + width * own_first, width), spot, :]
        for k, peer in enumerate(peers if s in direct else peers[:2]):
            hand_on(s, k, held, peer)

    def hand_on(s, k, held, peer):
        copy = remote(held, held, fin_s.at[s, k], fin_r.at[s, k], peer, ctx)
        copy.start()
        copies["fin", s, k] = copy

    def relay(s):
        low, width = slots[s]
        for k, (flip_fast, flip_slow) in enumerate(((1, 0), (0, 1))):
            copies["fin", s, k].wait_recv()
            their_fast = fast + flip_fast * (1 - 2 * fast)
            their_slow = slow + flip_slow * (1 - 2 * slow)
            first = jnp.where(top_half, their_fast, their_slow)
            second = jnp.where(top_half, their_slow, their_fast)
            if width == 2:
                held = gath.at[pl.ds(low + width * first + k, 1), pl.ds(pl.multiple_of(second * part, 16), part), :]
            else:
                spot = pl.ds(pl.multiple_of(second * part + k * (part // 2), 16), part // 2)
                held = gath.at[pl.ds(low + width * first, 1), spot, :]
            hand_on(s, 2 + k, held, peers[1 - k])

    def grad_in(r, low, high, last):
        rows_in = slice(r * 256, (r + 1) * 256)
        total = gi_acc[r] if low else jnp.zeros((256, tok_rows), F32)
        for p in range(low, high, 2):
            pairs = jnp.concatenate([comb[p], comb[p + 1]], axis=1)
            if p < HEADS:
                weight = wq[rows_in, p * HEAD_DIM : (p + 2) * HEAD_DIM]
            else:
                weight = jnp.concatenate([wkv[rows_in, c] for c in columns((p - HEADS) // 2)], axis=1)
            total = total + dot(weight, pairs, NT)
        if last:
            gi_ref[:, rows_in] = total.T.astype(BF)
        else:
            gi_acc[r] = total

    def tokens_in():
        for copy in tok_copies:
            copy.wait_recv()

    def grad_in_heads(r):
        grad_in(r, 0, HEADS, False)

    def grad_in_rest():
        for r in range(model // 256):
            grad_in(r, HEADS, COLUMNS, True)

    units = [(g, p, b) for g in range(KV_HEADS) for p in range(GROUP // 2) for b in reversed(range(blocks))]
    before = {(g, 0, b): step for g in range(KV_HEADS) for b, step in ((blocks - 1, near_halo), (0, far_halo))}
    after = {
        (0, 1, 0): ((send_slot, 0),),
        (0, 2, 0): ((send_halo, 0),),
        (1, 0, 0): ((send_slot, 1),),
    }
    scored, softened = {}, {}
    for t in range(len(units) + 2):
        if t < len(units):
            if units[t] in before:
                before[units[t]](units[t][0])
            scored[t] = score(units[t])
        if 0 <= t - 1 < len(units):
            softened[t - 1] = soften(units[t - 1], *scored.pop(t - 1))
        if t >= 2:
            derive(units[t - 2], *softened.pop(t - 2))
            for step, *operands in after.get(units[t - 2], ()):
                step(*operands)
    schedule = (
        (send_halo, 1), (tokens_in,), (multiply, 0), (finish_keyval, 0), (send_slot, 3), (halve, 0),
        (send_slot, 2), (multiply, 1), (halve, 1), (spread, 0), (multiply, 3), (finish_keyval, 1),
        (send_slot, 4), (halve, 3), (multiply, 2), (spread, 1), (halve, 2), (multiply, 4), (collect, 0),
        (halve, 4), (spread, 3), (collect, 1), (grad_in_heads, 0), (grad_in_heads, 1), (relay, 0),
        (spread, 2), (spread, 4), (grad_in_heads, 2), (grad_in_heads, 3), (relay, 1), (collect, 3),
        (grad_in_heads, 4), (grad_in_heads, 5), (grad_in_rest,), (relay, 3), (collect, 2), (collect, 4),
    )
    for step, *operands in schedule:
        step(*operands)
    for name, copy in copies.items():
        if name[0] == "fin" and (name[1] in direct or name[2] >= 2):
            copy.wait_recv()
    for j in range(COLUMNS):
        if j < HEADS:
            gwq_ref[:, j * HEAD_DIM : (j + 1) * HEAD_DIM] = gath[j]
        else:
            at = KV_HEADS * ((j - HEADS) % 2) + (j - HEADS) // 2
            gwkv_ref[:, at * HEAD_DIM : (at + 1) * HEAD_DIM] = gath[j]
    for copy in list(copies.values()) + tok_copies:
        copy.wait_send()
    for one, two in halo_copies:
        @pl.when(ctx + 1 < n_ctx)
        def _():
            one.wait_send()

        @pl.when(ctx + 2 < n_ctx)
        def _():
            two.wait_send()

    for g in range(KV_HEADS):
        for one, two in gh_copies[g]:
            @pl.when(ctx >= 1)
            def _():
                one.wait_send()

            @pl.when(ctx >= 2)
            def _():
                two.wait_send()


def copy_kernel(*refs):
    count = (len(refs) - 1) // 2
    sources, targets, sems = refs[:count], refs[count : 2 * count], refs[-1]
    leave = [pltpu.make_async_copy(sources[i], targets[i], sems.at[i]) for i in range(count)]
    for copy in leave:
        copy.start()
    for copy in leave:
        copy.wait()


def copied(arrays):
    hbm = pl.BlockSpec(memory_space=pltpu.MemorySpace.HBM)
    return pl.pallas_call(
        copy_kernel,
        out_shape=tuple(jax.ShapeDtypeStruct(a.shape, a.dtype) for a in arrays),
        in_specs=[pl.BlockSpec(memory_space=pl.ANY)] * len(arrays),
        out_specs=(hbm,) * len(arrays),
        scratch_shapes=[pltpu.SemaphoreType.DMA((len(arrays),))],
        compiler_params=pltpu.CompilerParams(vmem_limit_bytes=1024 * 1024),
        name="results",
    )(*arrays)


def square_scratch(n_ctx, tok_rows, model, kv_cols):
    n_z = n_ctx // 2
    n_h = n_z // 2
    rows = model // n_ctx
    part = rows // 2
    keys = HALO + tok_rows
    held = COLUMNS // 2
    dma = pltpu.SemaphoreType.DMA
    return [
        pltpu.VMEM((tok_rows, model), BF),
        pltpu.VMEM((1, n_ctx * tok_rows), jnp.int32),
        pltpu.VMEM((model, model), BF),
        pltpu.VMEM((model, kv_cols), BF),
        pltpu.VMEM((tok_rows, model), BF),
        pltpu.VMEM((2, 2, n_h * rows, tok_rows), BF),
        pltpu.VMEM((2, 2, n_h * rows, tok_rows), BF),
        pltpu.VMEM((HEADS, tok_rows, HEAD_DIM), BF),
        pltpu.VMEM((keys, kv_cols), BF),
        pltpu.VMEM((KV_HEADS, 2, HEAD_DIM, keys), BF),
        pltpu.VMEM((keys, BLOCK), jnp.int32),
        pltpu.VMEM((tok_rows // BLOCK, WINDOW, BLOCK), F32),
        pltpu.VMEM((keys, kv_cols), F32),
        pltpu.VMEM((HALO, kv_cols), BF),
        pltpu.VMEM((HALO, kv_cols), BF),
        pltpu.VMEM((COLUMNS, tok_rows, HEAD_DIM), BF),
        pltpu.VMEM((2, held, tok_rows, HEAD_DIM), BF),
        pltpu.VMEM((held, 2, n_h * rows, HEAD_DIM), BF),
        pltpu.VMEM((held, 2, n_h * rows, HEAD_DIM), BF),
        pltpu.VMEM((held, 2, n_h * rows, HEAD_DIM), F32),
        pltpu.VMEM((2, held, n_h, part, HEAD_DIM), BF),
        pltpu.VMEM((2, held, n_h, part, HEAD_DIM), BF),
        pltpu.VMEM((n_z, held, part, HEAD_DIM), BF),
        pltpu.VMEM((n_z - 1, held, part, HEAD_DIM), BF),
        pltpu.VMEM((COLUMNS, rows, HEAD_DIM), BF),
        pltpu.VMEM((model // 256, 256, tok_rows), F32),
        dma((5,)),
        dma((2,)), dma((2,)),
        dma((KV_HEADS, 2, 2)), dma((KV_HEADS, 2, 2)),
        dma((KV_HEADS, 2, 2)), dma((KV_HEADS, 2, 2)),
        dma((5, 2)), dma((5, 2)),
        dma((5,)), dma((5,)),
        dma((5, 2)), dma((5, 2)),
        dma((5, n_z - 1)), dma((5, n_z - 1)),
        dma((5, 4)), dma((5, 4)),
    ]


def shards(tokens, segments, w_query, w_keyval, grad_context):
    hidden_in = tokens[0]
    tok_rows, model = hidden_in.shape
    kv_cols = w_keyval.shape[1]
    n_ctx = lax.axis_size("ctx")
    n_dp = lax.axis_size("dp")
    n_z = n_ctx // 2
    rows = model // n_ctx
    slots = COLUMNS // n_dp
    half = n_z * rows
    square = n_dp == 4 and n_ctx % 4 == 0 and rows % 32 == 0
    keys = HALO + tok_rows
    vmem = pl.BlockSpec(memory_space=pltpu.VMEM)
    hbm = pl.BlockSpec(memory_space=pltpu.MemorySpace.HBM)
    dma = pltpu.SemaphoreType.DMA
    results = pl.pallas_call(
        functools.partial(square_kernel, n_ctx) if square else functools.partial(layer_kernel, n_dp, n_ctx),
        out_shape=(
            pltpu.VMEM((tok_rows, model), BF),
            pltpu.VMEM((tok_rows, model), BF),
            pltpu.VMEM((rows, model), BF),
            pltpu.VMEM((rows, kv_cols), BF),
        ),
        in_specs=[hbm, hbm if square else vmem, hbm, hbm, hbm],
        out_specs=(vmem,) * 4,
        scratch_shapes=square_scratch(n_ctx, tok_rows, model, kv_cols) if square else [
            pltpu.VMEM((tok_rows, model), BF),
            pltpu.VMEM((model, model), BF),
            pltpu.VMEM((model, kv_cols), BF),
            pltpu.VMEM((tok_rows, model), BF),
            pltpu.VMEM((n_dp, 2, half, tok_rows), BF),
            pltpu.VMEM((HEADS, tok_rows, HEAD_DIM), BF),
            pltpu.VMEM((keys, kv_cols), BF),
            pltpu.VMEM((keys, BLOCK), jnp.int32),
            pltpu.VMEM((keys, kv_cols), F32),
            pltpu.VMEM((HALO, kv_cols), BF),
            pltpu.VMEM((HALO, kv_cols), BF),
            pltpu.VMEM((COLUMNS, tok_rows, HEAD_DIM), BF),
            pltpu.VMEM((slots, n_dp - 1, tok_rows, HEAD_DIM), BF),
            pltpu.VMEM((slots, half, HEAD_DIM), BF),
            pltpu.VMEM((slots, half, HEAD_DIM), BF),
            pltpu.VMEM((slots, half, HEAD_DIM), F32),
            pltpu.VMEM((slots, half, HEAD_DIM), BF),
            pltpu.VMEM((slots, n_z - 1, rows, HEAD_DIM), BF),
            pltpu.VMEM((COLUMNS, rows, HEAD_DIM), BF),
            pltpu.VMEM((model // 256, 256, tok_rows), F32),
            dma((4,)),
            dma((n_dp - 1, 2)), dma((n_dp - 1, 2)),
            dma((KV_HEADS, 2, 2)), dma((KV_HEADS, 2, 2)),
            dma((KV_HEADS, 2, 2)), dma((KV_HEADS, 2, 2)),
            dma((slots, n_dp - 1)), dma((slots, n_dp - 1)),
            dma((slots,)), dma((slots,)),
            dma((slots, n_z - 1)), dma((slots, n_z - 1)),
            dma((slots, n_dp - 1)), dma((slots, n_dp - 1)),
        ],
        compiler_params=pltpu.CompilerParams(
            collective_id=0, has_side_effects=True, vmem_limit_bytes=61 * 1024 * 1024
        ),
        name="layer",
    )(hidden_in, segments, w_query, w_keyval, grad_context[0])
    context, grad_in, grad_wq, grad_wkv = copied(results)
    return context[None], grad_in[None], grad_wq, grad_wkv


def solution(mesh):
    placed = (P("dp", "ctx", None), P("dp", None), P(), P(), P("dp", "ctx", None))
    return jax.shard_map(
        shards,
        mesh=mesh,
        in_specs=placed,
        out_specs=(P("dp", "ctx", None), P("dp", "ctx", None), P("ctx", None), P("ctx", None)),
        check_vma=False,
    )
```
